128 devices in a mesh: band: 4 (over x), tile: 32 (over z, y, core).
Axes of the slice: x: 4, y: 4, z: 4, core: 2. Of those that a mesh axis runs over, the one named last changes fastest.
Arguments:
- obs_values: float32 [2, 32, 262144], P(None, None, ('band', 'tile')), may hold values from -6 to 6
- obs_place: float32 [3, 262144], P(None, ('band', 'tile')), as said below
- obs_depth: int32 [262144], P(('band', 'tile')), may hold values from 0 to 32, as said below
- node_place: float32 [2, 4096], P(None, 'tile'), as said below
- neighbours: int32 [4096, 1024], P('tile'), may hold values from 0 to 24575
- counts: int32 [4096], P('tile'), may hold values from 1 to 1024, as said below
Outputs:
- mapped: float32 [2, 32, 4096], P(None, 'band', 'tile')
The draws below stay inside these ranges and needn't reach their ends.
Inputs may be any that keep to these rules, and one draw needn't show every extreme that they name: `obs_place`: A profile in bucket j of its device's block (slots j * 64 to (j + 1) * 64 - 1) lies between longitudes -pi + j * 2 pi / 32 and -pi + (j + 1) * 2 pi / 32; latitudes lie within -1 and 1; the day angle within -pi and pi. `obs_depth`: 0 marks an empty slot; the first slot of every bucket holds a profile. `node_place`: the nodes of tile j lie between longitudes -pi + j * 2 pi / 32 and -pi + (j + 1) * 2 pi / 32, at latitudes within -1 and 1. `neighbours`: entries at list positions from counts[n] onward are padding. `counts`: the first node of every tile has a full list.
All inputs are finite; a program needn't handle non-finite values.
Results may differ from the reference program's by a relative error of at most 0.0003.
Values sent between devices are 32-bit elements; how exact they have to be, the bound alone decides.
A program may use at most 128 MiB of HBM per device.

```python
import math
import jax
import jax.numpy as jnp
from jax import lax

LEV = 32
K = 1024
CAP = 64
NODE_TILE = 128
PROFILES = 262144
NODES = 4096
N_BAND = 4
N_TILE = 32


def draw_obs_place(key, part):
    key_parts = jax.random.split(key, 3)
    tile_of = jnp.arange(PROFILES, dtype=jnp.int32) // CAP % N_TILE
    longitude = (tile_of.astype(jnp.float32) + jax.random.uniform(key_parts[0], (PROFILES,), jnp.float32)) * (2.0 * math.pi / N_TILE) - math.pi
    latitude = jax.random.uniform(key_parts[1], (PROFILES,), jnp.float32, -1.0, 1.0)
    day_angle = jax.random.uniform(key_parts[2], (PROFILES,), jnp.float32, -math.pi, math.pi)
    return jnp.stack([longitude, latitude, day_angle])


def draw_obs_depth(key, part):
    key_parts = jax.random.split(key, 4)
    slot_ids = jnp.arange(PROFILES, dtype=jnp.int32)
    tile_of = slot_ids // CAP % N_TILE
    rates = jax.random.randint(key_parts[0], (N_TILE,), 40, 101)
    occupied = jax.random.randint(key_parts[1], (PROFILES,), 0, 100) < rates[tile_of]
    full_depth = jax.random.randint(key_parts[2], (PROFILES,), 0, 10) < 6
    shallow = jax.random.randint(key_parts[3], (PROFILES,), 1, LEV + 1)
    depths = jnp.where(full_depth, LEV, shallow)
    depths = jnp.where(occupied | (slot_ids % CAP == 0), depths, 0)
    return depths.astype(jnp.int32)


def draw_node_place(key, part):
    key_parts = jax.random.split(key, 2)
    tile_of = jnp.arange(NODES, dtype=jnp.int32) // NODE_TILE
    longitude = (tile_of.astype(jnp.float32) + jax.random.uniform(key_parts[0], (NODES,), jnp.float32)) * (2.0 * math.pi / N_TILE) - math.pi
    latitude = jax.random.uniform(key_parts[1], (NODES,), jnp.float32, -1.0, 1.0)
    return jnp.stack([longitude, latitude])


def draw_counts(key, part):
    key_parts = jax.random.split(key, 2)
    node_ids = jnp.arange(NODES, dtype=jnp.int32)
    tile_of = node_ids // NODE_TILE
    factor = jax.random.randint(key_parts[0], (N_TILE,), 2, 9)
    drawn = 1 + jax.random.randint(key_parts[1], (NODES,), 0, K) * factor[tile_of] // 8
    return jnp.where(node_ids % NODE_TILE == 0, K, drawn).astype(jnp.int32)


def set_ends(result, stream_key, least, high):
    place = [jax.random.randint(jax.random.fold_in(stream_key, axis), (), 0, length) for axis, length in enumerate(result.shape)]
    main_axis = result.shape.index(max(result.shape))
    beside = place[:main_axis] + [(place[main_axis] + 1) % result.shape[main_axis]] + place[main_axis + 1:]
    return result.at[tuple(place)].set(least).at[tuple(beside)].set(high)


def block_scale(rng, dims, cuts, least, high):
    def one(dim, parts):
        steps = jax.random.uniform(jax.random.fold_in(jax.random.fold_in(rng, 6), dim), (parts,), jnp.float32, least / len(cuts), high / len(cuts))
        return jnp.repeat(jnp.exp(steps), dims[dim] // parts).reshape((-1,) + (1,) * (len(dims) - dim - 1))

    gain = one(*cuts[0])
    for cut in cuts[1:]:
        gain = gain * one(*cut)
    return gain


def bell_draw(stream_key, extent, deviation, bound, shards=(), held_as=jnp.bfloat16):
    loudness = block_scale(stream_key, extent, shards, -0.22, 0.18) if shards else 1.0
    values = jax.random.normal(stream_key, extent, jnp.float32) * deviation * loudness
    return jnp.minimum(jnp.maximum(values, -bound), bound).astype(held_as)


def setup_inputs(seed: int = 0) -> dict:
    key_list = jax.random.split(jax.random.key(seed), 7)
    obs_values = bell_draw(key_list[0], (2, LEV, PROFILES), 1.0, 6.0, ((2, 128),), jnp.float32)
    obs_place = draw_obs_place(jax.random.fold_in(key_list[6], 71), 0)
    obs_depth = draw_obs_depth(jax.random.fold_in(key_list[6], 71), 0)
    node_place = draw_node_place(jax.random.fold_in(key_list[6], 71), 0)
    neighbours = set_ends(jax.random.randint(key_list[4], (NODES, K), 0, 3 * CAP * N_BAND * N_TILE), jax.random.fold_in(key_list[4], 1), 0, (3 * CAP * N_BAND * N_TILE) - 1).astype(jnp.int32)
    counts = draw_counts(jax.random.fold_in(key_list[6], 71), 0)
    return dict(obs_values=obs_values, obs_place=obs_place, obs_depth=obs_depth, node_place=node_place, neighbours=neighbours, counts=counts)


SPREAD = 0.5
RIDGE_WEIGHT = 1.0
MONTH_ANGLE = -11.0 * math.pi / 12.0
BASIS_PAIRS = [(first_index, second_index) for first_index in range(5) for second_index in range(first_index, 5)]
HIGHEST = lax.Precision.HIGHEST

def profile_rows(obs_place, obs_depth):
    longitude, latitude, day_angle = (obs_place[0], obs_place[1], obs_place[2])
    cos_lat = jnp.cos(latitude)
    return jnp.stack([cos_lat * jnp.cos(longitude), cos_lat * jnp.sin(longitude), jnp.sin(latitude), jnp.cos(day_angle), jnp.sin(day_angle), obs_depth.astype(jnp.float32)])

def node_frames(longitude, latitude):
    sin_lat, cos_lat = (jnp.sin(latitude), jnp.cos(latitude))
    sin_lon, cos_lon = (jnp.sin(longitude), jnp.cos(longitude))
    return [cos_lat * cos_lon, cos_lat * sin_lon, sin_lat, -sin_lon, cos_lon, -sin_lat * cos_lon, -sin_lat * sin_lon, cos_lat]

def block_terms(picked, node_frame, valid_mask, level_ids):
    levels = level_ids.shape[0]
    unit_x, unit_y, unit_z = (picked[2 * levels], picked[2 * levels + 1], picked[2 * levels + 2])
    node_x, node_y, node_z, east_x, east_y, north_x, north_y, north_z = node_frame
    chord_sq = (unit_x - node_x) ** 2 + (unit_y - node_y) ** 2 + (unit_z - node_z) ** 2
    weight = jnp.exp(-chord_sq / (SPREAD * SPREAD)) * valid_mask
    east_off = (unit_x * east_x + unit_y * east_y) / SPREAD
    north_off = (unit_x * north_x + unit_y * north_y + unit_z * north_z) / SPREAD
    basis_rows = [jnp.ones_like(weight), east_off, north_off, picked[2 * levels + 3], picked[2 * levels + 4]]
    depth_rows = picked[2 * levels + 5]
    inside = (level_ids[:, None, None] < depth_rows[None]).astype(jnp.float32)
    crossed = jnp.stack([weight * basis_rows[left_index] * basis_rows[right_index] for left_index, right_index in BASIS_PAIRS])
    normal = jnp.einsum('pnk,lnk->pln', crossed, inside, precision=HIGHEST)
    values = picked[:2 * levels].reshape(2, levels, picked.shape[1], picked.shape[2]) * inside[None]
    weighted = jnp.stack([weight * basis_one for basis_one in basis_rows])
    moments = jnp.einsum('pnk,vlnk->pvln', weighted, values, precision=HIGHEST)
    return (normal, moments)

def solve_fit(normal, moments):
    position = {}
    for place_index, pair in enumerate(BASIS_PAIRS):
        position[pair] = place_index
    lower = {}
    for column in range(5):
        diagonal = normal[position[column, column]] + RIDGE_WEIGHT
        for inner in range(column):
            diagonal = diagonal - lower[column, inner] * lower[column, inner]
        pivot_root = jnp.sqrt(diagonal)
        lower[column, column] = pivot_root
        for target in range(column + 1, 5):
            element = normal[position[column, target]]
            for inner in range(column):
                element = element - lower[target, inner] * lower[column, inner]
            lower[target, column] = element / pivot_root
    forward = []
    for target in range(5):
        residue = moments[target]
        for inner in range(target):
            residue = residue - lower[target, inner] * forward[inner]
        forward.append(residue / lower[target, target])
    coeffs = [None] * 5
    for target in reversed(range(5)):
        residue = forward[target]
        for inner in range(target + 1, 5):
            residue = residue - lower[inner, target] * coeffs[inner]
        coeffs[target] = residue / lower[target, target]
    return coeffs[0] + coeffs[3] * math.cos(MONTH_ANGLE) + coeffs[4] * math.sin(MONTH_ANGLE)

def reference(obs_values, obs_place, obs_depth, node_place, neighbours, counts):
    devices = N_BAND * N_TILE
    merged = jnp.concatenate([obs_values.reshape(2 * LEV, PROFILES), profile_rows(obs_place, obs_depth)], axis=0)
    row_count = merged.shape[0]
    by_tile = merged.reshape(row_count, devices, N_TILE, CAP).transpose(2, 0, 1, 3).reshape(N_TILE, row_count, devices * CAP)
    level_ids = jnp.arange(LEV, dtype=jnp.int32).astype(jnp.float32)
    frames_all = node_frames(node_place[0], node_place[1])
    node_step = math.gcd(NODE_TILE, 128)

    def one_tile(tile_id):
        extended = jnp.concatenate([by_tile[(tile_id + N_TILE - 1) % N_TILE], by_tile[tile_id], by_tile[(tile_id + 1) % N_TILE]], axis=1)

        def one_block(block_id):
            start_row = tile_id * NODE_TILE + block_id * node_step
            lists_block = lax.dynamic_slice_in_dim(neighbours, start_row, node_step, 0)
            count_block = lax.dynamic_slice_in_dim(counts, start_row, node_step, 0)
            frame_block = [lax.dynamic_slice_in_dim(part_rows, start_row, node_step, 0)[:, None] for part_rows in frames_all]
            picked = jnp.take(extended, lists_block, axis=1)
            valid_mask = (jnp.arange(K, dtype=jnp.int32)[None, :] < count_block[:, None]).astype(jnp.float32)
            normal, moments = block_terms(picked, frame_block, valid_mask, level_ids)
            return solve_fit(normal, moments)
        blocks = lax.map(one_block, jnp.arange(NODE_TILE // node_step, dtype=jnp.int32))
        return blocks.transpose(1, 2, 0, 3).reshape(2, LEV, NODE_TILE)
    tiles_out = lax.map(one_tile, jnp.arange(N_TILE, dtype=jnp.int32))
    return tiles_out.transpose(1, 2, 0, 3).reshape(2, LEV, NODES)
```

```python
import math

import jax
import jax.numpy as jnp
from jax import lax
from jax.experimental import pallas as pl
from jax.experimental.pallas import tpu as pltpu
from jax.sharding import PartitionSpec as P

MONTH_ANGLE = -11.0 * math.pi / 12.0
BF = jnp.bfloat16
F32 = jnp.float32
E4 = jnp.float8_e4m3fn
NT_DIMS = (((1,), (1,)), ((), ()))
LANES = 128
GROUPS = 19
VMEM_LIMIT = 60 * 2**20


def list_rows(nb_ref, cnt_ref, hi_ref, lo_ref):
    nb = nb_ref[...]
    valid = lax.broadcasted_iota(jnp.int32, nb.shape, 1) < cnt_ref[...]
    hi_ref[...] = jnp.where(valid, lax.shift_right_logical(nb, 7), -1).astype(F32)
    lo_ref[...] = lax.bitwise_and(nb, LANES - 1).astype(F32)


def count_node(n, hi_ref, lo_ref, m_ref):
    fan = hi_ref.shape[1]
    tiles = m_ref.shape[1]
    hi_ids = lax.broadcasted_iota(jnp.int32, (tiles, fan), 0).astype(BF)
    lo_ids = lax.broadcasted_iota(jnp.int32, (LANES, fan), 0).astype(BF)
    hi = jnp.broadcast_to(hi_ref[pl.ds(n, 1), :], (16, fan)).astype(BF)
    lo = jnp.broadcast_to(lo_ref[pl.ds(n, 1), :], (16, fan)).astype(BF)
    hi = jnp.concatenate([hi] * (tiles // 16), 0)
    lo = jnp.concatenate([lo] * (LANES // 16), 0)
    one, zero = jnp.ones((), BF), jnp.zeros((), BF)
    hot_hi = jnp.where(hi_ids == hi, one, zero).astype(E4)
    hot_lo = jnp.where(lo_ids == lo, one, zero).astype(E4)
    m_ref[pl.ds(n, 1)] = lax.dot_general(hot_hi, hot_lo, NT_DIMS, preferred_element_type=F32)[None]


def split2(x):
    high = x.astype(BF)
    return high, (x - high.astype(F32)).astype(BF)


def split3(x):
    high = x.astype(BF)
    rest = x - high.astype(F32)
    mid = rest.astype(BF)
    return high, mid, (rest - mid.astype(F32)).astype(BF)


def node_left(node_x, node_y, node_z):
    scale = 8.0 * math.log2(math.e)
    col = lax.broadcasted_iota(jnp.int32, (node_x.shape[0], LANES), 1)
    row = lax.bitwise_and(col, 7)
    vals = jnp.where(
        row == 0,
        node_x * scale,
        jnp.where(row == 1, node_y * scale, jnp.where(row == 2, node_z * scale, jnp.where(row == 6, -scale, 0.0))),
    )
    high, mid, low = split3(vals)
    block = lax.shift_right_logical(col, 3)
    high, mid, low = high.astype(F32), mid.astype(F32), low.astype(F32)
    part = jnp.where(
        (block == 0) | (block == 3) | (block == 5),
        high,
        jnp.where((block == 1) | (block == 4), mid, jnp.where(block == 2, low, 0.0)),
    )
    return part.astype(BF)


def meta_features(meta):
    dense = jnp.swapaxes(meta, 0, 1)
    x, y, z, c, s = (dense[i] for i in range(5))
    return [x, y, z, c, s, x * x, x * y, x * z, y * y, y * z, x * c, y * c, z * c, x * s, y * s, z * s, c * c, c * s]


def ext_block(blk, level_base, ext_ref, m_ref, left, gh_ref, gl_ref, fh_ref, fl_ref, acc_ref):
    nodes = m_ref.shape[0]
    start = pl.multiple_of(blk * 8, 8)
    meta = ext_ref[pl.ds(start, 8), 16:24, :]
    prods = meta_features(meta)
    for index, prod in enumerate(prods):
        high = prod.astype(BF).astype(F32)
        gh_ref[index] = high
        gl_ref[index] = prod - high
    level = (lax.broadcasted_iota(jnp.int32, (8, LANES), 0) + level_base).astype(F32)
    zero = jnp.zeros((8, LANES), F32)
    profile_parts = []
    for t in range(8):
        cols = pl.ds(t * LANES, LANES)
        rows = ext_ref[start + t]
        tile_meta = rows[16:24]
        inside = level < jnp.broadcast_to(tile_meta[5:6], (8, LANES))
        high, mid, low = split3(tile_meta)
        high, mid, low = high.astype(F32), mid.astype(F32), low.astype(F32)
        profile_parts.append(jnp.concatenate([high, high, high, mid, mid, low], 0).astype(BF))
        highs = [jnp.where(inside, 1.0, 0.0)]
        lows = [zero]
        for index in range(GROUPS - 1):
            highs.append(jnp.where(inside, jnp.broadcast_to(gh_ref[index, t : t + 1, :], (8, LANES)), zero))
            lows.append(jnp.where(inside, jnp.broadcast_to(gl_ref[index, t : t + 1, :], (8, LANES)), zero))
        factors = [jnp.broadcast_to(tile_meta[i : i + 1], (8, LANES)) for i in range(5)]
        for v in range(2):
            value = jnp.where(inside, rows[8 * v : 8 * v + 8], zero)
            for term in [value] + [value * factor for factor in factors]:
                high = term.astype(BF).astype(F32)
                highs.append(high)
                lows.append(term - high)
        highs.append(zero)
        lows.append(zero)
        for pair in range(16):
            part = pl.ds(pair * 16, 16)
            fh_ref[part, cols] = jnp.concatenate(highs[2 * pair : 2 * pair + 2], 0).astype(BF)
            fl_ref[part, cols] = jnp.concatenate(lows[2 * pair : 2 * pair + 2], 0).astype(BF)
    right = jnp.concatenate(profile_parts, 1)
    power = lax.dot_general(left[:, :48], right, (((1,), (0,)), ((), ())), preferred_element_type=F32)
    counted = m_ref[:, pl.ds(start, 8), :]
    counted = jnp.swapaxes(counted.reshape(nodes // 8, 8, 8, LANES), 1, 2)
    counted = jnp.concatenate([counted[:, t].reshape(nodes, LANES) for t in range(8)], 1)
    weight = jnp.exp2(power) * counted
    w_high, w_low = split2(weight)
    both = jnp.concatenate([w_high, w_low], 0)
    first = lax.dot_general(fh_ref[...], both, NT_DIMS, preferred_element_type=F32)
    second = lax.dot_general(fl_ref[...], w_high, NT_DIMS, preferred_element_type=F32)
    acc_ref[...] += first[:, :nodes] + first[:, nodes:] + second


def fit_nodes(acc_ref, frame, out_ref):
    nodes = acc_ref.shape[1]
    ex, ey, qx, qy, qz = (jnp.broadcast_to(2.0 * part, (8, nodes)) for part in frame)
    sums = [acc_ref[8 * i : 8 * i + 8, :] for i in range(GROUPS + 12)]
    s1, sx, sy, sz, sc, ss, sxx, sxy, sxz, syy, syz, sxc, syc, szc, sxs, sys_, szs, scc, scs = sums[:GROUPS]
    szz = s1 - sxx - syy
    normal = {
        (0, 0): s1,
        (0, 1): ex * sx + ey * sy,
        (0, 2): qx * sx + qy * sy + qz * sz,
        (0, 3): sc,
        (0, 4): ss,
        (1, 1): ex * ex * sxx + 2.0 * ex * ey * sxy + ey * ey * syy,
        (1, 2): ex * qx * sxx + (ex * qy + ey * qx) * sxy + ey * qy * syy + ex * qz * sxz + ey * qz * syz,
        (1, 3): ex * sxc + ey * syc,
        (1, 4): ex * sxs + ey * sys_,
        (2, 2): qx * qx * sxx + qy * qy * syy + qz * qz * szz + 2.0 * (qx * qy * sxy + qx * qz * sxz + qy * qz * syz),
        (2, 3): qx * sxc + qy * syc + qz * szc,
        (2, 4): qx * sxs + qy * sys_ + qz * szs,
        (3, 3): scc,
        (3, 4): scs,
        (4, 4): s1 - scc,
    }
    lower = {}
    inverse = []
    for column in range(5):
        diagonal = normal[column, column] + 1.0
        for inner in range(column):
            diagonal = diagonal - lower[column, inner] * lower[column, inner]
        inverse.append(1.0 / jnp.sqrt(diagonal))
        for target in range(column + 1, 5):
            element = normal[column, target]
            for inner in range(column):
                element = element - lower[target, inner] * lower[column, inner]
            lower[target, column] = element * inverse[column]
    for v in range(2):
        m1, mx, my, mz, mc, ms = sums[GROUPS + 6 * v : GROUPS + 6 * v + 6]
        moments = [m1, ex * mx + ey * my, qx * mx + qy * my + qz * mz, mc, ms]
        forward = []
        for target in range(5):
            residue = moments[target]
            for inner in range(target):
                residue = residue - lower[target, inner] * forward[inner]
            forward.append(residue * inverse[target])
        coeffs = [None] * 5
        for target in reversed(range(5)):
            residue = forward[target]
            for inner in range(target + 1, 5):
                residue = residue - lower[inner, target] * coeffs[inner]
            coeffs[target] = residue * inverse[target]
        out_ref[v] = coeffs[0] + coeffs[3] * math.cos(MONTH_ANGLE) + coeffs[4] * math.sin(MONTH_ANGLE)


def node_frame(longitude, latitude):
    sin_lat, cos_lat = jnp.sin(latitude), jnp.cos(latitude)
    sin_lon, cos_lon = jnp.sin(longitude), jnp.cos(longitude)
    point = (cos_lat * cos_lon, cos_lat * sin_lon, sin_lat)
    frame = (-sin_lon, cos_lon, -sin_lat * cos_lon, -sin_lat * sin_lon, cos_lat)
    return point, frame


def fit_kernel(nb_ref, cnt_ref, place_ref, place_t_ref, ext_ref, out_ref, hi_ref, lo_ref, m_ref, gh_ref, gl_ref, fh_ref, fl_ref, acc_ref):
    nodes = nb_ref.shape[0]
    list_rows(nb_ref, cnt_ref, hi_ref, lo_ref)

    def count_step(n, carry):
        count_node(n, hi_ref, lo_ref, m_ref)
        return carry

    lax.fori_loop(0, nodes, count_step, 0, unroll=8)
    acc_ref[...] = jnp.zeros_like(acc_ref)
    point, _ = node_frame(place_t_ref[:, 0:1], place_t_ref[:, 1:2])
    left = node_left(*point)
    level_base = lax.axis_index("band") * 8

    def block_step(blk, carry):
        ext_block(blk, level_base, ext_ref, m_ref, left, gh_ref, gl_ref, fh_ref, fl_ref, acc_ref)
        return carry

    lax.fori_loop(0, m_ref.shape[1] // 8, block_step, 0)
    _, frame = node_frame(place_ref[0:1, :], place_ref[1:2, :])
    fit_nodes(acc_ref, frame, out_ref)


def fit_call(neighbours, counts, node_place, ext):
    nodes, fan = neighbours.shape
    tiles = ext.shape[0]
    vmem = pl.BlockSpec(memory_space=pltpu.VMEM)
    return pl.pallas_call(
        fit_kernel,
        out_shape=jax.ShapeDtypeStruct((2, 8, nodes), F32),
        in_specs=[vmem] * 5,
        out_specs=vmem,
        scratch_shapes=[
            pltpu.VMEM((nodes, fan), F32),
            pltpu.VMEM((nodes, fan), F32),
            pltpu.VMEM((nodes, tiles, LANES), F32),
            pltpu.VMEM((GROUPS - 1, 8, LANES), F32),
            pltpu.VMEM((GROUPS - 1, 8, LANES), F32),
            pltpu.VMEM((256, 8 * LANES), BF),
            pltpu.VMEM((256, 8 * LANES), BF),
            pltpu.VMEM((256, nodes), F32),
        ],
        compiler_params=pltpu.CompilerParams(vmem_limit_bytes=VMEM_LIMIT),
    )(neighbours, counts.reshape(nodes, 1), node_place, node_place.T, ext)


def profile_rows(obs_place, obs_depth):
    longitude, latitude, day_angle = obs_place[0], obs_place[1], obs_place[2]
    cos_lat = jnp.cos(latitude)
    return jnp.stack(
        [
            cos_lat * jnp.cos(longitude),
            cos_lat * jnp.sin(longitude),
            jnp.sin(latitude),
            jnp.cos(day_angle),
            jnp.sin(day_angle),
            obs_depth.astype(F32),
            jnp.ones_like(longitude),
            jnp.zeros_like(longitude),
        ]
    )


def body(obs_values, obs_place, obs_depth, node_place, neighbours, counts):
    bands = lax.axis_size("band")
    tiles = lax.axis_size("tile")
    levels = obs_values.shape[1] // bands
    slots = obs_values.shape[2] // tiles
    values = obs_values.reshape(2, bands, levels, tiles, slots).transpose(1, 3, 0, 2, 4).reshape(bands, tiles, 2 * levels, slots)
    meta = profile_rows(obs_place, obs_depth).reshape(8, tiles, slots).transpose(1, 0, 2)
    meta = jnp.broadcast_to(meta[None], (bands,) + meta.shape)
    rows = jnp.concatenate([values, meta], 2).reshape(bands * tiles, 2 * levels + 8, slots)
    got = lax.all_to_all(rows, ("band", "tile"), 0, 0, tiled=True)
    devices = got.shape[0]
    got = got.reshape(devices // 2, 2, 2 * levels + 8, slots).transpose(0, 2, 1, 3).reshape(devices // 2, 2 * levels + 8, 2 * slots)
    forward = [(i, (i + 1) % tiles) for i in range(tiles)]
    backward = [(t, s) for s, t in forward]
    low = lax.ppermute(got, "tile", forward)
    high = lax.ppermute(got, "tile", backward)
    ext = jnp.concatenate([low, got, high], 0)
    return fit_call(neighbours, counts, node_place, ext)


def solution(mesh):
    return jax.shard_map(
        body,
        mesh=mesh,
        in_specs=(
            P(None, None, ("band", "tile")),
            P(None, ("band", "tile")),
            P(("band", "tile")),
            P(None, "tile"),
            P("tile", None),
            P("tile"),
        ),
        out_specs=P(None, "band", "tile"),
        check_vma=False,
    )
```

```python
import math

import jax
import jax.numpy as jnp
from jax import lax
from jax.experimental import pallas as pl
from jax.experimental.pallas import tpu as pltpu
from jax.sharding import PartitionSpec as P

MONTH_ANGLE = -11.0 * math.pi / 12.0
BF = jnp.bfloat16
F32 = jnp.float32
E4 = jnp.float8_e4m3fn
NT_DIMS = (((1,), (1,)), ((), ()))
LANES = 128
MESH = pl.DeviceIdType.MESH
GROUPS = 19
VMEM_LIMIT = 60 * 2**20


def list_rows(core, nb_ref, cnt_col, hi_ref, lo_ref):
    nb = nb_ref[...]
    valid = lax.broadcasted_iota(jnp.int32, nb.shape, 1).astype(F32) < cnt_col
    segment = lax.shift_right_logical(nb, 13)
    chip = lax.bitwise_and(lax.shift_right_logical(nb, 7), 63)
    source_core = lax.bitwise_and(lax.shift_right_logical(nb, 6), 1)
    slot = chip_slot(lax.shift_right_logical(chip, 4), lax.bitwise_and(lax.shift_right_logical(chip, 2), 3), lax.bitwise_and(chip, 3))
    is_halo = segment == 2 * core
    half = segment - 1 + core
    hi = slot + jnp.where(is_halo, 128, jnp.where(source_core == core, 0, 64))
    lo = jnp.where(is_halo, lax.bitwise_and(nb, 127), lax.bitwise_and(nb, 63) + 64 * half)
    hi_ref[...] = jnp.where(valid, hi, -1).astype(F32)
    lo_ref[...] = lo.astype(F32)


def chip_slot(x, z, y):
    return lax.bitwise_and(x + z + y, 3) * 16 + x * 4 + y


def count_node(n, hi_ref, lo_ref, m_ref):
    fan = hi_ref.shape[1]
    tiles = m_ref.shape[1]
    hi_ids = lax.broadcasted_iota(jnp.int32, (tiles, fan), 0).astype(BF)
    lo_ids = lax.broadcasted_iota(jnp.int32, (LANES, fan), 0).astype(BF)
    hi = jnp.broadcast_to(hi_ref[pl.ds(n, 1), :], (16, fan)).astype(BF)
    lo = jnp.broadcast_to(lo_ref[pl.ds(n, 1), :], (16, fan)).astype(BF)
    hi = jnp.concatenate([hi] * (tiles // 16), 0)
    lo = jnp.concatenate([lo] * (LANES // 16), 0)
    one, zero = jnp.ones((), BF), jnp.zeros((), BF)
    hot_hi = jnp.where(hi_ids == hi, one, zero).astype(E4)
    hot_lo = jnp.where(lo_ids == lo, one, zero).astype(E4)
    m_ref[pl.ds(n, 1)] = lax.dot_general(hot_hi, hot_lo, NT_DIMS, preferred_element_type=F32)[None]


def split2(x):
    high = x.astype(BF)
    return high, (x - high.astype(F32)).astype(BF)


def split3(x):
    high = x.astype(BF)
    rest = x - high.astype(F32)
    mid = rest.astype(BF)
    return high, mid, (rest - mid.astype(F32)).astype(BF)


def node_left(node_x, node_y, node_z):
    scale = 8.0 * math.log2(math.e)
    col = lax.broadcasted_iota(jnp.int32, (node_x.shape[0], LANES), 1)
    row = lax.bitwise_and(col, 7)
    vals = jnp.where(
        row == 0,
        node_x * scale,
        jnp.where(row == 1, node_y * scale, jnp.where(row == 2, node_z * scale, jnp.where(row == 6, -scale, 0.0))),
    )
    high, mid, low = split3(vals)
    block = lax.shift_right_logical(col, 3)
    high, mid, low = high.astype(F32), mid.astype(F32), low.astype(F32)
    part = jnp.where(
        (block == 0) | (block == 3) | (block == 5),
        high,
        jnp.where((block == 1) | (block == 4), mid, jnp.where(block == 2, low, 0.0)),
    )
    return part.astype(BF)


def meta_features(meta):
    dense = jnp.swapaxes(meta, 0, 1)
    x, y, z, c, s = (dense[i] for i in range(5))
    return [x, y, z, c, s, x * x, x * y, x * z, y * y, y * z, x * c, y * c, z * c, x * s, y * s, z * s, c * c, c * s]


def ext_block(blk, level_base, ext_ref, m_ref, left, gh_ref, gl_ref, fh_ref, fl_ref, acc_ref):
    nodes = m_ref.shape[0]
    start = pl.multiple_of(blk * 8, 8)
    meta = ext_ref[pl.ds(start, 8), 16:24, :]
    prods = meta_features(meta)
    for index, prod in enumerate(prods):
        high = prod.astype(BF).astype(F32)
        gh_ref[index] = high
        gl_ref[index] = prod - high
    level = (lax.broadcasted_iota(jnp.int32, (8, LANES), 0) + level_base).astype(F32)
    zero = jnp.zeros((8, LANES), F32)
    profile_parts = []
    for t in range(8):
        cols = pl.ds(t * LANES, LANES)
        rows = ext_ref[start + t]
        tile_meta = rows[16:24]
        inside = level < jnp.broadcast_to(tile_meta[5:6], (8, LANES))
        high, mid, low = split3(tile_meta)
        high, mid, low = high.astype(F32), mid.astype(F32), low.astype(F32)
        profile_parts.append(jnp.concatenate([high, high, high, mid, mid, low], 0).astype(BF))
        highs = [jnp.where(inside, 1.0, 0.0)]
        lows = [zero]
        for index in range(GROUPS - 1):
            highs.append(jnp.where(inside, jnp.broadcast_to(gh_ref[index, t : t + 1, :], (8, LANES)), zero))
            lows.append(jnp.where(inside, jnp.broadcast_to(gl_ref[index, t : t + 1, :], (8, LANES)), zero))
        factors = [jnp.broadcast_to(tile_meta[i : i + 1], (8, LANES)) for i in range(5)]
        for v in range(2):
            value = jnp.where(inside, rows[8 * v : 8 * v + 8], zero)
            for term in [value] + [value * factor for factor in factors]:
                high = term.astype(BF).astype(F32)
                highs.append(high)
                lows.append(term - high)
        highs.append(zero)
        lows.append(zero)
        for pair in range(16):
            part = pl.ds(pair * 16, 16)
            fh_ref[part, cols] = jnp.concatenate(highs[2 * pair : 2 * pair + 2], 0).astype(BF)
            fl_ref[part, cols] = jnp.concatenate(lows[2 * pair : 2 * pair + 2], 0).astype(BF)
    right = jnp.concatenate(profile_parts, 1)
    power = lax.dot_general(left[:, :48], right, (((1,), (0,)), ((), ())), preferred_element_type=F32)
    counted = m_ref[:, pl.ds(start, 8), :]
    counted = jnp.swapaxes(counted.reshape(nodes // 8, 8, 8, LANES), 1, 2)
    counted = jnp.concatenate([counted[:, t].reshape(nodes, LANES) for t in range(8)], 1)
    weight = jnp.exp2(power) * counted
    w_high, w_low = split2(weight)
    both = jnp.concatenate([w_high, w_low], 0)
    first = lax.dot_general(fh_ref[...], both, NT_DIMS, preferred_element_type=F32)
    second = lax.dot_general(fl_ref[...], w_high, NT_DIMS, preferred_element_type=F32)
    acc_ref[...] += first[:, :nodes] + first[:, nodes:] + second


def fit_nodes(acc_ref, frame, out_ref):
    nodes = acc_ref.shape[1]
    ex, ey, qx, qy, qz = (jnp.broadcast_to(2.0 * part, (8, nodes)) for part in frame)
    sums = [acc_ref[8 * i : 8 * i + 8, :] for i in range(GROUPS + 12)]
    s1, sx, sy, sz, sc, ss, sxx, sxy, sxz, syy, syz, sxc, syc, szc, sxs, sys_, szs, scc, scs = sums[:GROUPS]
    szz = s1 - sxx - syy
    normal = {
        (0, 0): s1,
        (0, 1): ex * sx + ey * sy,
        (0, 2): qx * sx + qy * sy + qz * sz,
        (0, 3): sc,
        (0, 4): ss,
        (1, 1): ex * ex * sxx + 2.0 * ex * ey * sxy + ey * ey * syy,
        (1, 2): ex * qx * sxx + (ex * qy + ey * qx) * sxy + ey * qy * syy + ex * qz * sxz + ey * qz * syz,
        (1, 3): ex * sxc + ey * syc,
        (1, 4): ex * sxs + ey * sys_,
        (2, 2): qx * qx * sxx + qy * qy * syy + qz * qz * szz + 2.0 * (qx * qy * sxy + qx * qz * sxz + qy * qz * syz),
        (2, 3): qx * sxc + qy * syc + qz * szc,
        (2, 4): qx * sxs + qy * sys_ + qz * szs,
        (3, 3): scc,
        (3, 4): scs,
        (4, 4): s1 - scc,
    }
    lower = {}
    inverse = []
    for column in range(5):
        diagonal = normal[column, column] + 1.0
        for inner in range(column):
            diagonal = diagonal - lower[column, inner] * lower[column, inner]
        inverse.append(1.0 / jnp.sqrt(diagonal))
        for target in range(column + 1, 5):
            element = normal[column, target]
            for inner in range(column):
                element = element - lower[target, inner] * lower[column, inner]
            lower[target, column] = element * inverse[column]
    for v in range(2):
        m1, mx, my, mz, mc, ms = sums[GROUPS + 6 * v : GROUPS + 6 * v + 6]
        moments = [m1, ex * mx + ey * my, qx * mx + qy * my + qz * mz, mc, ms]
        forward = []
        for target in range(5):
            residue = moments[target]
            for inner in range(target):
                residue = residue - lower[target, inner] * forward[inner]
            forward.append(residue * inverse[target])
        coeffs = [None] * 5
        for target in reversed(range(5)):
            residue = forward[target]
            for inner in range(target + 1, 5):
                residue = residue - lower[inner, target] * coeffs[inner]
            coeffs[target] = residue * inverse[target]
        out_ref[v] = coeffs[0] + coeffs[3] * math.cos(MONTH_ANGLE) + coeffs[4] * math.sin(MONTH_ANGLE)


def node_frame(longitude, latitude):
    sin_lat, cos_lat = jnp.sin(latitude), jnp.cos(latitude)
    sin_lon, cos_lon = jnp.sin(longitude), jnp.cos(longitude)
    point = (cos_lat * cos_lon, cos_lat * sin_lon, sin_lat)
    frame = (-sin_lon, cos_lon, -sin_lat * cos_lon, -sin_lat * sin_lon, cos_lat)
    return point, frame


def dense_rows(ref, row):
    return jnp.concatenate([ref[row : row + 1, m * LANES : (m + 1) * LANES] for m in range(ref.shape[1] // LANES)], 0)


def profile_meta(place_ref, depth_ref):
    longitude, latitude, day_angle = (dense_rows(place_ref, row) for row in range(3))
    cos_lat = jnp.cos(latitude)
    rows = [
        cos_lat * jnp.cos(longitude),
        cos_lat * jnp.sin(longitude),
        jnp.sin(latitude),
        jnp.cos(day_angle),
        jnp.sin(day_angle),
        dense_rows(depth_ref, 0).astype(F32),
        jnp.ones_like(cos_lat),
        jnp.zeros_like(cos_lat),
    ]
    return jnp.swapaxes(jnp.stack(rows, 0), 0, 1)


def full_kernel(
    values_ref, place_ref, depth_ref, node_ref, nb_ref, cnt_ref, out_ref,
    meta_ref, sib_values_ref, sib_meta_ref, own_ref, halo_ref, ext_ref,
    hi_ref, lo_ref, m_ref, gh_ref, gl_ref, fh_ref, fl_ref, acc_ref,
    send_own, send_halo, recv, pass_send, sib_send, sib_recv,
):
    x = lax.axis_index("band")
    tile = lax.axis_index("tile")
    core = lax.rem(tile, 2)
    chip = lax.div(tile, 2)
    z, y = lax.div(chip, 4), lax.rem(chip, 4)
    sibling = {"tile": tile + 1 - 2 * core}
    mine = chip_slot(x, z, y)
    phase = lax.rem(x + z + y, 4)
    nodes = nb_ref.shape[0]

    def partner(index):
        dx, dy = lax.rem(lax.div(index, 4), 4), lax.rem(index, 4)
        dz = lax.rem(lax.div(index, 16) + 8 - dx - dy, 4)
        other_x, other_z, other_y = lax.rem(x + dx, 4), lax.rem(z + dz, 4), lax.rem(y + dy, 4)
        pair = other_z * 4 + other_y
        return other_x * 16 + pair, {"band": other_x, "tile": 2 * pair + core}

    barrier = pltpu.get_barrier_semaphore()

    def greet(index, carry):
        _, device = partner(index)
        pl.semaphore_signal(barrier, inc=1, device_id=device, device_id_type=MESH)
        return carry

    lax.fori_loop(1, 64, greet, 0)
    pl.semaphore_signal(barrier, inc=1, device_id=sibling, device_id_type=MESH)

    meta_ref[...] = profile_meta(place_ref, depth_ref)
    for b in range(4):
        for m in range(16):
            for v in range(2):
                own_ref[b * 16 + m, 8 * v : 8 * v + 8, :] = values_ref[v, 8 * b : 8 * b + 8, m * LANES : (m + 1) * LANES]
            own_ref[b * 16 + m, 16:24, :] = meta_ref[m]
    point, frame = node_frame(node_ref[0:1, :], node_ref[1:2, :])
    packed = jnp.concatenate(list(point) + [cnt_ref[...].astype(F32)] + [jnp.zeros((124, nodes), F32)], 0)
    columns = packed.T
    left = node_left(columns[:, 0:1], columns[:, 1:2], columns[:, 2:3])
    list_rows(core, nb_ref, columns[:, 3:4], hi_ref, lo_ref)
    acc_ref[...] = jnp.zeros_like(acc_ref)

    pl.semaphore_wait(barrier, 64)
    sib_copies = [
        pltpu.make_async_remote_copy(values_ref, sib_values_ref, sib_send.at[0], sib_recv.at[0], device_id=sibling, device_id_type=MESH),
        pltpu.make_async_remote_copy(meta_ref, sib_meta_ref, sib_send.at[1], sib_recv.at[1], device_id=sibling, device_id_type=MESH),
    ]
    for copy in sib_copies:
        copy.start()

    def send(buffer, base, send_sem):
        def step(index, carry):
            unit, device = partner(index)
            pltpu.make_async_remote_copy(
                buffer.at[unit], ext_ref.at[16 * base + mine], send_sem, recv.at[base + phase], device_id=device, device_id_type=MESH
            ).start()
            return carry

        lax.fori_loop(1, 64, step, 0)

    def keep(buffer, base):
        return pltpu.make_async_copy(buffer.at[x * 16 + chip], ext_ref.at[16 * base + mine], recv.at[base + phase])

    def group(index):
        return ext_ref.at[pl.ds(pl.multiple_of(index * 16, 16), 16)]

    def wait_group(index):
        pltpu.make_async_copy(group(index), group(index), recv.at[index]).wait()

    keep(own_ref, 0).start()
    send(own_ref, 0, send_own)

    def send_halos():
        for copy in sib_copies:
            copy.wait_recv()
        from_own = lax.shift_right_logical(lax.broadcasted_iota(jnp.int32, (8, LANES), 1), 6) == core

        def step(m, carry):
            other = lax.rem(m + 15 + 2 * core, 16)
            cols = pl.ds(pl.multiple_of(other * LANES, LANES), LANES)
            meta = jnp.where(from_own, pltpu.roll(meta_ref[other], 64, 1), sib_meta_ref[other])
            for b in range(4):
                unit = b * 16 + m
                for v in range(2):
                    mine_rows = values_ref[v, 8 * b : 8 * b + 8, cols]
                    their_rows = sib_values_ref[v, 8 * b : 8 * b + 8, cols]
                    halo_ref[unit, 8 * v : 8 * v + 8, :] = jnp.where(from_own, pltpu.roll(mine_rows, 64, 1), their_rows)
                halo_ref[unit, 16:24, :] = meta
            return carry

        lax.fori_loop(0, 16, step, 0)
        keep(halo_ref, 8).start()
        send(halo_ref, 8, send_halo)

    def pass_copy(k):
        return pltpu.make_async_remote_copy(
            group(k), group(4 + k), pass_send.at[k], recv.at[4 + k], device_id=sibling, device_id_type=MESH
        )

    def pass_group(order):
        k = lax.rem(phase + 4 - order, 4)
        wait_group(k)
        pass_copy(k).start()

    def count_step(step, carry):
        for n in range(8):
            count_node(step * 8 + n, hi_ref, lo_ref, m_ref)
        pl.when(step == 1)(send_halos)
        pl.when((step >= 9) & (lax.rem(step, 2) == 1))(lambda: pass_group(lax.div(step - 9, 2)))
        return carry

    lax.fori_loop(0, nodes // 8, count_step, 0)
    level_base = x * 8

    def pair_step(pair, carry):
        k = lax.rem(phase + 4 - lax.rem(pair, 4), 4)
        index = lax.div(pair, 4) * 4 + k
        pl.when(pair >= 4)(lambda: wait_group(index))

        def block_step(part, inner):
            ext_block(2 * index + part, level_base, ext_ref, m_ref, left, gh_ref, gl_ref, fh_ref, fl_ref, acc_ref)
            return inner

        return lax.fori_loop(0, 2, block_step, carry)

    lax.fori_loop(0, 12, pair_step, 0)
    fit_nodes(acc_ref, frame, out_ref)
    for buffer, send_sem in ((own_ref, send_own), (halo_ref, send_halo)):
        view = buffer.at[pl.ds(0, 63)]
        pltpu.make_async_copy(view, view, send_sem).wait()
    for k in range(4):
        pass_copy(k).wait_send()
    for copy in sib_copies:
        copy.wait_send()


def body(obs_values, obs_place, obs_depth, node_place, neighbours, counts):
    nodes, fan = neighbours.shape
    vmem = pl.BlockSpec(memory_space=pltpu.VMEM)
    dma = pltpu.SemaphoreType.DMA
    return pl.pallas_call(
        full_kernel,
        out_shape=jax.ShapeDtypeStruct((2, 8, nodes), F32),
        in_specs=[vmem] * 6,
        out_specs=vmem,
        scratch_shapes=[
            pltpu.VMEM((16, 8, LANES), F32),
            pltpu.VMEM(obs_values.shape, F32),
            pltpu.VMEM((16, 8, LANES), F32),
            pltpu.VMEM((64, 24, LANES), F32),
            pltpu.VMEM((64, 24, LANES), F32),
            pltpu.VMEM((192, 24, LANES), F32),
            pltpu.VMEM((nodes, fan), F32),
            pltpu.VMEM((nodes, fan), F32),
            pltpu.VMEM((nodes, 192, LANES), F32),
            pltpu.VMEM((GROUPS - 1, 8, LANES), F32),
            pltpu.VMEM((GROUPS - 1, 8, LANES), F32),
            pltpu.VMEM((256, 8 * LANES), BF),
            pltpu.VMEM((256, 8 * LANES), BF),
            pltpu.VMEM((256, nodes), F32),
            dma,
            dma,
            dma((12,)),
            dma((4,)),
            dma((2,)),
            dma((2,)),
        ],
        compiler_params=pltpu.CompilerParams(vmem_limit_bytes=VMEM_LIMIT, collective_id=0, has_side_effects=True),
    )(obs_values, obs_place, obs_depth.reshape(1, -1), node_place, neighbours, counts.reshape(1, nodes))


def solution(mesh):
    return jax.shard_map(
        body,
        mesh=mesh,
        in_specs=(
            P(None, None, ("band", "tile")),
            P(None, ("band", "tile")),
            P(("band", "tile")),
            P(None, "tile"),
            P("tile", None),
            P("tile"),
        ),
        out_specs=P(None, "band", "tile"),
        check_vma=False,
    )
```

```python
import math

import jax
import jax.numpy as jnp
from jax import lax
from jax.experimental import pallas as pl
from jax.experimental.pallas import tpu as pltpu
from jax.sharding import PartitionSpec as P

MONTH_ANGLE = -11.0 * math.pi / 12.0
BF = jnp.bfloat16
F32 = jnp.float32
E4 = jnp.float8_e4m3fn
I8 = jnp.int8
NT_DIMS = (((1,), (1,)), ((), ()))
LANES = 128
MESH = pl.DeviceIdType.MESH
GROUPS = 19
VMEM_LIMIT = 60 * 2**20


def list_rows(core, nb_ref, cnt_col, hi_ref, lo_ref):
    nb = nb_ref[...]
    valid = lax.broadcasted_iota(jnp.int32, nb.shape, 1).astype(F32) < cnt_col
    segment = lax.shift_right_logical(nb, 13)
    chip = lax.bitwise_and(lax.shift_right_logical(nb, 7), 63)
    source_core = lax.bitwise_and(lax.shift_right_logical(nb, 6), 1)
    slot = chip_slot(lax.shift_right_logical(chip, 4), lax.bitwise_and(lax.shift_right_logical(chip, 2), 3), lax.bitwise_and(chip, 3))
    is_halo = segment == 2 * core
    half = segment - 1 + core
    hi = slot + jnp.where(is_halo, 64, jnp.where(source_core == core, -64, 0))
    lo = jnp.where(is_halo, lax.bitwise_and(nb, 127), lax.bitwise_and(nb, 63) + 64 * half)
    hi_ref[...] = jnp.where(valid, hi, -128)
    lo_ref[...] = lo


def chip_slot(x, z, y):
    return lax.bitwise_and(x + z + y, 3) * 16 + x * 4 + y


def count_nodes(step, hi_ref, lo_ref, tmp_ref):
    fan = hi_ref.shape[1]
    tiles = tmp_ref.shape[1]
    hi_ids = (lax.broadcasted_iota(jnp.int32, (tiles, fan), 0) - 64).astype(I8)
    lo_ids = lax.broadcasted_iota(jnp.int32, (LANES, fan), 0).astype(I8)
    one, zero = jnp.ones((), E4), jnp.zeros((), E4)
    for i in range(8):
        n = step * 8 + i
        hi = jnp.broadcast_to(hi_ref[pl.ds(n, 1), :], (32, fan)).astype(I8)
        lo = jnp.broadcast_to(lo_ref[pl.ds(n, 1), :], (32, fan)).astype(I8)
        hot_hi = jnp.where(hi_ids == jnp.concatenate([hi] * (tiles // 32), 0), one, zero)
        hot_lo = jnp.where(lo_ids == jnp.concatenate([lo] * (LANES // 32), 0), one, zero)
        tmp_ref[i] = lax.dot_general(hot_hi, hot_lo, NT_DIMS, preferred_element_type=F32)


def place_counts(step, tmp_ref, m_ref):
    m_ref[:, pl.ds(pl.multiple_of(step * 8, 8), 8), :] = jnp.swapaxes(tmp_ref[...], 0, 1)


def split2(x):
    high = x.astype(BF)
    return high, (x - high.astype(F32)).astype(BF)


def split3(x):
    high = x.astype(BF)
    rest = x - high.astype(F32)
    mid = rest.astype(BF)
    return high, mid, (rest - mid.astype(F32)).astype(BF)


def node_left(node_x, node_y, node_z):
    scale = 8.0 * math.log2(math.e)
    col = lax.broadcasted_iota(jnp.int32, (node_x.shape[0], LANES), 1)
    row = lax.bitwise_and(col, 7)
    vals = jnp.where(
        row == 0,
        node_x * scale,
        jnp.where(row == 1, node_y * scale, jnp.where(row == 2, node_z * scale, jnp.where(row == 6, -scale, 0.0))),
    )
    high, mid, low = split3(vals)
    block = lax.shift_right_logical(col, 3)
    high, mid, low = high.astype(F32), mid.astype(F32), low.astype(F32)
    part = jnp.where(
        (block == 0) | (block == 3) | (block == 5),
        high,
        jnp.where((block == 1) | (block == 4), mid, jnp.where(block == 2, low, 0.0)),
    )
    return part.astype(BF)


def meta_features(meta):
    dense = jnp.swapaxes(meta, 0, 1)
    x, y, z, c, s = (dense[i] for i in range(5))
    return [x, y, z, c, s, x * x, x * y, x * z, y * y, y * z, x * c, y * c, z * c, x * s, y * s, z * s, c * c, c * s]


def build_block(blk, level_base, ext_ref, m_ref, left, gh_ref, gl_ref, fh_ref, fl_ref, w_ref):
    nodes = m_ref.shape[1]
    start = pl.multiple_of(blk * 8, 8)
    meta = ext_ref[pl.ds(start, 8), 16:24, :]
    for index, prod in enumerate(meta_features(meta)):
        high = prod.astype(BF).astype(F32)
        gh_ref[index] = high
        gl_ref[index] = prod - high
    row = lax.broadcasted_iota(jnp.int32, (16, LANES), 0)
    level = (lax.bitwise_and(row, 7) + level_base).astype(F32)
    level16 = level.astype(BF)
    zero, one = jnp.zeros((8, LANES), F32), jnp.ones((8, LANES), F32)
    zero16 = jnp.zeros((16, LANES), BF)
    parts = []
    for t in range(8):
        cols = pl.ds(t * LANES, LANES)
        rows = ext_ref[start + t]
        tile_meta = rows[16:24]
        depth = jnp.broadcast_to(tile_meta[5:6], (8, LANES))
        inside = level[0:8] < depth
        inside16 = level16 < jnp.concatenate([depth, depth], 0).astype(BF)
        high, mid, low = split3(tile_meta)
        high, mid, low = high.astype(F32), mid.astype(F32), low.astype(F32)
        parts.append(jnp.concatenate([high, high, high, mid, mid, low], 0).astype(BF))
        for g_ref, f_ref, first in ((gh_ref, fh_ref, one), (gl_ref, fl_ref, zero)):
            terms = [first] + [jnp.broadcast_to(g_ref[i, t : t + 1, :], (8, LANES)) for i in range(GROUPS - 1)] + [zero]
            for pair in range(10):
                both = jnp.concatenate(terms[2 * pair : 2 * pair + 2], 0).astype(BF)
                f_ref[pl.ds(pair * 16, 16), cols] = jnp.where(inside16, both, zero16)
        factors = [jnp.broadcast_to(tile_meta[i : i + 1], (8, LANES)) for i in range(5)]
        for v in range(2):
            value = jnp.where(inside, rows[8 * v : 8 * v + 8], zero)
            terms = [value] + [value * factor for factor in factors]
            for pair in range(3):
                both = jnp.concatenate(terms[2 * pair : 2 * pair + 2], 0)
                high = both.astype(BF)
                part = pl.ds((10 + 3 * v + pair) * 16, 16)
                fh_ref[part, cols] = high
                fl_ref[part, cols] = (both - high.astype(F32)).astype(BF)
    right = jnp.concatenate(parts, 1)
    power = lax.dot_general(left[:, :48], right, (((1,), (0,)), ((), ())), preferred_element_type=F32)
    for t in range(8):
        cols = pl.ds(t * LANES, LANES)
        w_high, w_low = split2(jnp.exp2(power[:, t * LANES : (t + 1) * LANES]) * m_ref[start + t])
        w_ref[0:nodes, cols] = w_high
        w_ref[nodes:, cols] = w_low


def add_block(fh_ref, fl_ref, w_ref, acc_ref):
    nodes = acc_ref.shape[1]
    first = lax.dot_general(fh_ref[...], w_ref[...], NT_DIMS, preferred_element_type=F32)
    second = lax.dot_general(fl_ref[...], w_ref[0:nodes, :], NT_DIMS, preferred_element_type=F32)
    acc_ref[...] += first[:, :nodes] + first[:, nodes:] + second


def fit_nodes(acc_ref, frame, out_ref):
    nodes = acc_ref.shape[1]
    ex, ey, qx, qy, qz = (jnp.broadcast_to(2.0 * part, (8, nodes)) for part in frame)
    sums = [acc_ref[8 * i : 8 * i + 8, :] for i in range(32)]
    del sums[GROUPS]
    s1, sx, sy, sz, sc, ss, sxx, sxy, sxz, syy, syz, sxc, syc, szc, sxs, sys_, szs, scc, scs = sums[:GROUPS]
    szz = s1 - sxx - syy
    normal = {
        (0, 0): s1,
        (0, 1): ex * sx + ey * sy,
        (0, 2): qx * sx + qy * sy + qz * sz,
        (0, 3): sc,
        (0, 4): ss,
        (1, 1): ex * ex * sxx + 2.0 * ex * ey * sxy + ey * ey * syy,
        (1, 2): ex * qx * sxx + (ex * qy + ey * qx) * sxy + ey * qy * syy + ex * qz * sxz + ey * qz * syz,
        (1, 3): ex * sxc + ey * syc,
        (1, 4): ex * sxs + ey * sys_,
        (2, 2): qx * qx * sxx + qy * qy * syy + qz * qz * szz + 2.0 * (qx * qy * sxy + qx * qz * sxz + qy * qz * syz),
        (2, 3): qx * sxc + qy * syc + qz * szc,
        (2, 4): qx * sxs + qy * sys_ + qz * szs,
        (3, 3): scc,
        (3, 4): scs,
        (4, 4): s1 - scc,
    }
    lower = {}
    inverse = []
    for column in range(5):
        diagonal = normal[column, column] + 1.0
        for inner in range(column):
            diagonal = diagonal - lower[column, inner] * lower[column, inner]
        inverse.append(1.0 / jnp.sqrt(diagonal))
        for target in range(column + 1, 5):
            element = normal[column, target]
            for inner in range(column):
                element = element - lower[target, inner] * lower[column, inner]
            lower[target, column] = element * inverse[column]
    for v in range(2):
        m1, mx, my, mz, mc, ms = sums[GROUPS + 6 * v : GROUPS + 6 * v + 6]
        moments = [m1, ex * mx + ey * my, qx * mx + qy * my + qz * mz, mc, ms]
        forward = []
        for target in range(5):
            residue = moments[target]
            for inner in range(target):
                residue = residue - lower[target, inner] * forward[inner]
            forward.append(residue * inverse[target])
        coeffs = [None] * 5
        for target in reversed(range(5)):
            residue = forward[target]
            for inner in range(target + 1, 5):
                residue = residue - lower[inner, target] * coeffs[inner]
            coeffs[target] = residue * inverse[target]
        out_ref[v] = coeffs[0] + coeffs[3] * math.cos(MONTH_ANGLE) + coeffs[4] * math.sin(MONTH_ANGLE)


def node_frame(longitude, latitude):
    sin_lat, cos_lat = jnp.sin(latitude), jnp.cos(latitude)
    sin_lon, cos_lon = jnp.sin(longitude), jnp.cos(longitude)
    point = (cos_lat * cos_lon, cos_lat * sin_lon, sin_lat)
    frame = (-sin_lon, cos_lon, -sin_lat * cos_lon, -sin_lat * sin_lon, cos_lat)
    return point, frame


def dense_rows(ref, row):
    return jnp.concatenate([ref[row : row + 1, m * LANES : (m + 1) * LANES] for m in range(ref.shape[1] // LANES)], 0)


def profile_meta(place_ref, depth_ref):
    longitude, latitude, day_angle = (dense_rows(place_ref, row) for row in range(3))
    cos_lat = jnp.cos(latitude)
    rows = [
        cos_lat * jnp.cos(longitude),
        cos_lat * jnp.sin(longitude),
        jnp.sin(latitude),
        jnp.cos(day_angle),
        jnp.sin(day_angle),
        dense_rows(depth_ref, 0).astype(F32),
        jnp.ones_like(cos_lat),
        jnp.zeros_like(cos_lat),
    ]
    return jnp.swapaxes(jnp.stack(rows, 0), 0, 1)


def compute(nodes, level_base, before_count, before_pair, left, ext_ref, hi_ref, lo_ref, m_ref, work):
    tmp_a, tmp_b, gh_a, gl_a, gh_b, gl_b, fh_a, fl_a, w_a, fh_b, fl_b, w_b, acc_ref = work
    acc_ref[...] = jnp.zeros_like(acc_ref)
    count_nodes(0, hi_ref, lo_ref, tmp_a)
    last = nodes // 16 - 1

    def count_step(step, carry):
        before_count(step)
        count_nodes(2 * step + 1, hi_ref, lo_ref, tmp_b)
        place_counts(2 * step, tmp_a, m_ref)
        count_nodes(2 * step + 2, hi_ref, lo_ref, tmp_a)
        place_counts(2 * step + 1, tmp_b, m_ref)
        return carry

    lax.fori_loop(0, last, count_step, 0)
    before_count(last)
    count_nodes(2 * last + 1, hi_ref, lo_ref, tmp_b)
    place_counts(2 * last, tmp_a, m_ref)
    place_counts(2 * last + 1, tmp_b, m_ref)

    def build(blk, gh_ref, gl_ref, fh_ref, fl_ref, w_ref):
        build_block(blk, level_base, ext_ref, m_ref, left, gh_ref, gl_ref, fh_ref, fl_ref, w_ref)

    set_a = (gh_a, gl_a, fh_a, fl_a, w_a)
    set_b = (gh_b, gl_b, fh_b, fl_b, w_b)
    index = before_pair(0)
    build(2 * index, *set_a)

    def pair_step(pair, index):
        following = before_pair(pair + 1)
        build(2 * index + 1, *set_b)
        add_block(fh_a, fl_a, w_a, acc_ref)
        build(2 * following, *set_a)
        add_block(fh_b, fl_b, w_b, acc_ref)
        return following

    pairs = ext_ref.shape[0] // 16
    index = lax.fori_loop(0, pairs - 1, pair_step, index)
    build(2 * index + 1, *set_b)
    add_block(fh_a, fl_a, w_a, acc_ref)
    add_block(fh_b, fl_b, w_b, acc_ref)


def work_buffers(nodes):
    tile = pltpu.VMEM((8, 192, LANES), F32)
    dense = pltpu.VMEM((GROUPS - 1, 8, LANES), F32)
    wide = pltpu.VMEM((256, 8 * LANES), BF)
    return (tile, tile) + (dense,) * 4 + (wide,) * 6 + (pltpu.VMEM((256, nodes), F32),)


def full_kernel(
    values_ref, place_ref, depth_ref, node_ref, nb_ref, cnt_ref, out_ref,
    meta_ref, sib_values_ref, sib_meta_ref, own_ref, halo_ref, ext_ref,
    hi_ref, lo_ref, m_ref, work,
    send_own, send_halo, recv, pass_send, sib_send, sib_recv,
):
    x = lax.axis_index("band")
    tile = lax.axis_index("tile")
    core = lax.rem(tile, 2)
    chip = lax.div(tile, 2)
    z, y = lax.div(chip, 4), lax.rem(chip, 4)
    sibling = {"tile": tile + 1 - 2 * core}
    mine = chip_slot(x, z, y)
    phase = lax.rem(x + z + y, 4)
    nodes = nb_ref.shape[0]

    def partner(index):
        dx, dy = lax.bitwise_and(lax.shift_right_logical(index, 2), 3), lax.bitwise_and(index, 3)
        dz = lax.shift_right_logical(index, 4) + 8 - dx - dy
        other_x, other_z, other_y = lax.bitwise_and(x + dx, 3), lax.bitwise_and(z + dz, 3), lax.bitwise_and(y + dy, 3)
        pair = other_z * 4 + other_y
        return other_x * 16 + pair, {"band": other_x, "tile": 2 * pair + core}

    barrier = pltpu.get_barrier_semaphore()

    def greet(index, carry):
        _, device = partner(index)
        pl.semaphore_signal(barrier, inc=1, device_id=device, device_id_type=MESH)
        return carry

    lax.fori_loop(1, 64, greet, 0)
    pl.semaphore_signal(barrier, inc=1, device_id=sibling, device_id_type=MESH)

    meta_ref[...] = profile_meta(place_ref, depth_ref)
    for b in range(4):
        for m in range(16):
            for v in range(2):
                own_ref[b * 16 + m, 8 * v : 8 * v + 8, :] = values_ref[v, 8 * b : 8 * b + 8, m * LANES : (m + 1) * LANES]
            own_ref[b * 16 + m, 16:24, :] = meta_ref[m]
    point, frame = node_frame(node_ref[0:1, :], node_ref[1:2, :])
    packed = jnp.concatenate(list(point) + [cnt_ref[...].astype(F32)] + [jnp.zeros((124, nodes), F32)], 0)
    columns = packed.T
    left = node_left(columns[:, 0:1], columns[:, 1:2], columns[:, 2:3])
    list_rows(core, nb_ref, columns[:, 3:4], hi_ref, lo_ref)

    pl.semaphore_wait(barrier, 64)
    sib_copies = [
        pltpu.make_async_remote_copy(values_ref, sib_values_ref, sib_send.at[0], sib_recv.at[0], device_id=sibling, device_id_type=MESH),
        pltpu.make_async_remote_copy(meta_ref, sib_meta_ref, sib_send.at[1], sib_recv.at[1], device_id=sibling, device_id_type=MESH),
    ]
    for copy in sib_copies:
        copy.start()

    def send(buffer, base, send_sem):
        def step(index, carry):
            unit, device = partner(index)
            pltpu.make_async_remote_copy(
                buffer.at[unit], ext_ref.at[16 * base + mine], send_sem, recv.at[base + phase], device_id=device, device_id_type=MESH
            ).start()
            return carry

        lax.fori_loop(1, 64, step, 0)

    def keep(buffer, base):
        return pltpu.make_async_copy(buffer.at[x * 16 + chip], ext_ref.at[16 * base + mine], recv.at[base + phase])

    def group(index):
        return ext_ref.at[pl.ds(pl.multiple_of(index * 16, 16), 16)]

    def wait_group(index):
        pltpu.make_async_copy(group(index), group(index), recv.at[index]).wait()

    keep(own_ref, 0).start()
    send(own_ref, 0, send_own)

    def send_halos():
        for copy in sib_copies:
            copy.wait_recv()
        from_own = lax.shift_right_logical(lax.broadcasted_iota(jnp.int32, (8, LANES), 1), 6) == core

        def step(m, carry):
            other = lax.rem(m + 15 + 2 * core, 16)
            cols = pl.ds(pl.multiple_of(other * LANES, LANES), LANES)
            meta = jnp.where(from_own, pltpu.roll(meta_ref[other], 64, 1), sib_meta_ref[other])
            for b in range(4):
                unit = b * 16 + m
                for v in range(2):
                    mine_rows = values_ref[v, 8 * b : 8 * b + 8, cols]
                    their_rows = sib_values_ref[v, 8 * b : 8 * b + 8, cols]
                    halo_ref[unit, 8 * v : 8 * v + 8, :] = jnp.where(from_own, pltpu.roll(mine_rows, 64, 1), their_rows)
                halo_ref[unit, 16:24, :] = meta
            return carry

        lax.fori_loop(0, 16, step, 0)
        keep(halo_ref, 8).start()
        send(halo_ref, 8, send_halo)

    def pass_copy(k):
        return pltpu.make_async_remote_copy(
            group(k), group(4 + k), pass_send.at[k], recv.at[4 + k], device_id=sibling, device_id_type=MESH
        )

    def pass_group(order):
        k = lax.rem(phase + 4 - order, 4)
        wait_group(k)
        pass_copy(k).start()

    def before_count(step):
        pl.when(step == 1)(send_halos)
        pl.when(step >= 4)(lambda: pass_group(step - 4))

    def before_pair(pair):
        k = lax.rem(phase + 4 - lax.rem(pair, 4), 4)
        index = lax.div(pair, 4) * 4 + k
        pl.when(pair >= 4)(lambda: wait_group(index))
        return index

    compute(nodes, x * 8, before_count, before_pair, left, ext_ref, hi_ref, lo_ref, m_ref, work)
    fit_nodes(work[-1], frame, out_ref)
    for buffer, send_sem in ((own_ref, send_own), (halo_ref, send_halo)):
        view = buffer.at[pl.ds(0, 63)]
        pltpu.make_async_copy(view, view, send_sem).wait()
    for k in range(4):
        pass_copy(k).wait_send()
    for copy in sib_copies:
        copy.wait_send()


def body(obs_values, obs_place, obs_depth, node_place, neighbours, counts):
    nodes, fan = neighbours.shape
    vmem = pl.BlockSpec(memory_space=pltpu.VMEM)
    dma = pltpu.SemaphoreType.DMA
    return pl.pallas_call(
        full_kernel,
        out_shape=jax.ShapeDtypeStruct((2, 8, nodes), F32),
        in_specs=[vmem] * 6,
        out_specs=vmem,
        scratch_shapes=[
            pltpu.VMEM((16, 8, LANES), F32),
            pltpu.VMEM(obs_values.shape, F32),
            pltpu.VMEM((16, 8, LANES), F32),
            pltpu.VMEM((64, 24, LANES), F32),
            pltpu.VMEM((64, 24, LANES), F32),
            pltpu.VMEM((192, 24, LANES), F32),
            pltpu.VMEM((nodes, fan), jnp.int32),
            pltpu.VMEM((nodes, fan), jnp.int32),
            pltpu.VMEM((192, nodes, LANES), F32),
            work_buffers(nodes),
            dma,
            dma,
            dma((12,)),
            dma((4,)),
            dma((2,)),
            dma((2,)),
        ],
        compiler_params=pltpu.CompilerParams(vmem_limit_bytes=VMEM_LIMIT, collective_id=0, has_side_effects=True),
    )(obs_values, obs_place, obs_depth.reshape(1, -1), node_place, neighbours, counts.reshape(1, nodes))


def solution(mesh):
    return jax.shard_map(
        body,
        mesh=mesh,
        in_specs=(
            P(None, None, ("band", "tile")),
            P(None, ("band", "tile")),
            P(("band", "tile")),
            P(None, "tile"),
            P("tile", None),
            P("tile"),
        ),
        out_specs=P(None, "band", "tile"),
        check_vma=False,
    )
```

```python
import math

import jax
import jax.numpy as jnp
from jax import lax
from jax.experimental import pallas as pl
from jax.experimental.pallas import tpu as pltpu
from jax.sharding import PartitionSpec as P

MONTH_ANGLE = -11.0 * math.pi / 12.0
BF = jnp.bfloat16
F32 = jnp.float32
E4 = jnp.float8_e4m3fn
I8 = jnp.int8
NT_DIMS = (((1,), (1,)), ((), ()))
LANES = 128
MESH = pl.DeviceIdType.MESH
GROUPS = 19
EARLY = 2
VMEM_LIMIT = 60 * 2**20


def list_rows(core, nb_ref, cnt_col, hi_ref, lo_ref):
    nb = nb_ref[...]
    valid = lax.broadcasted_iota(jnp.int32, nb.shape, 1).astype(F32) < cnt_col
    segment = lax.shift_right_logical(nb, 13)
    chip = lax.bitwise_and(lax.shift_right_logical(nb, 7), 63)
    source_core = lax.bitwise_and(lax.shift_right_logical(nb, 6), 1)
    slot = chip_slot(lax.shift_right_logical(chip, 4), lax.bitwise_and(lax.shift_right_logical(chip, 2), 3), lax.bitwise_and(chip, 3))
    is_halo = segment == 2 * core
    half = segment - 1 + core
    hi = slot + jnp.where(is_halo, 64, jnp.where(source_core == core, -64, 0))
    lo = jnp.where(is_halo, lax.bitwise_and(nb, 127), lax.bitwise_and(nb, 63) + 64 * half)
    hi_ref[...] = jnp.where(valid, hi, -128)
    lo_ref[...] = lo


def chip_slot(x, z, y):
    return lax.bitwise_and(x + z + y, 3) * 16 + x * 4 + y


def count_nodes(step, hi_ref, lo_ref, tmp_ref, last_ref, m_ref):
    fan = hi_ref.shape[1]
    tiles = tmp_ref.shape[1]
    hi_ids = (lax.broadcasted_iota(jnp.int32, (tiles, fan), 0) - 64).astype(I8)
    lo_ids = lax.broadcasted_iota(jnp.int32, (LANES, fan), 0).astype(I8)
    one, zero = jnp.ones((), E4), jnp.zeros((), E4)
    for i in range(8):
        n = step * 8 + i
        hi = jnp.broadcast_to(hi_ref[pl.ds(n, 1), :], (32, fan)).astype(I8)
        lo = jnp.broadcast_to(lo_ref[pl.ds(n, 1), :], (32, fan)).astype(I8)
        hot_hi = jnp.where(hi_ids == jnp.concatenate([hi] * (tiles // 32), 0), one, zero)
        hot_lo = jnp.where(lo_ids == jnp.concatenate([lo] * (LANES // 32), 0), one, zero)
        tmp_ref[i] = lax.dot_general(hot_hi, hot_lo, NT_DIMS, preferred_element_type=F32)
        if last_ref is not None:
            place_counts(step - 1, last_ref, m_ref, i * tiles // 8, (i + 1) * tiles // 8)


def place_counts(step, tmp_ref, m_ref, first, stop):
    m_ref[first:stop, pl.ds(pl.multiple_of(step * 8, 8), 8), :] = jnp.swapaxes(tmp_ref[:, first:stop, :], 0, 1)


def split2(x):
    high = x.astype(BF)
    return high, (x - high.astype(F32)).astype(BF)


def split3(x):
    high = x.astype(BF)
    rest = x - high.astype(F32)
    mid = rest.astype(BF)
    return high, mid, (rest - mid.astype(F32)).astype(BF)


def node_left(node_x, node_y, node_z):
    scale = 8.0 * math.log2(math.e)
    col = lax.broadcasted_iota(jnp.int32, (node_x.shape[0], LANES), 1)
    row = lax.bitwise_and(col, 7)
    vals = jnp.where(
        row == 0,
        node_x * scale,
        jnp.where(row == 1, node_y * scale, jnp.where(row == 2, node_z * scale, jnp.where(row == 6, -scale, 0.0))),
    )
    high, mid, low = split3(vals)
    block = lax.shift_right_logical(col, 3)
    high, mid, low = high.astype(F32), mid.astype(F32), low.astype(F32)
    part = jnp.where(
        (block == 0) | (block == 3) | (block == 5),
        high,
        jnp.where((block == 1) | (block == 4), mid, jnp.where(block == 2, low, 0.0)),
    )
    return part.astype(BF)


def meta_features(meta):
    dense = jnp.swapaxes(meta, 0, 1)
    x, y, z, c, s = (dense[i] for i in range(5))
    return [x, y, z, c, s, x * x, x * y, x * z, y * y, y * z, x * c, y * c, z * c, x * s, y * s, z * s, c * c, c * s]


def build_block(blk, level_base, ext_ref, gh_ref, gl_ref, fh_ref, fl_ref):
    start = pl.multiple_of(blk * 8, 8)
    meta = ext_ref[pl.ds(start, 8), 16:24, :]
    for index, prod in enumerate(meta_features(meta)):
        high = prod.astype(BF).astype(F32)
        gh_ref[index] = high
        gl_ref[index] = prod - high
    level = (lax.broadcasted_iota(jnp.int32, (8, LANES), 0) + level_base).astype(F32)
    zero, one = jnp.zeros((8, LANES), F32), jnp.ones((8, LANES), F32)
    parts = []
    for t in range(8):
        rows = ext_ref[start + t]
        tile_meta = rows[16:24]
        depth = jnp.broadcast_to(tile_meta[5:6], (8, LANES))
        inside = level < depth
        hold = jnp.where(inside, one, zero)
        high, mid, low = split3(tile_meta)
        high, mid, low = high.astype(F32), mid.astype(F32), low.astype(F32)
        parts.append(jnp.concatenate([high, high, high, mid, mid, low], 0).astype(BF))
        for g_ref, f_ref, first in ((gh_ref, fh_ref, hold), (gl_ref, fl_ref, zero)):
            terms = [jnp.where(inside, jnp.broadcast_to(g_ref[i, t : t + 1, :], (8, LANES)), zero) for i in range(GROUPS - 1)]
            terms = [first] + terms + [zero]
            for pair in range(10):
                f_ref[t, pl.ds(pair * 16, 16)] = jnp.concatenate(terms[2 * pair : 2 * pair + 2], 0).astype(BF)
        factors = [jnp.broadcast_to(tile_meta[i : i + 1], (8, LANES)) for i in range(5)]
        for v in range(2):
            value = jnp.where(inside, rows[8 * v : 8 * v + 8], zero)
            terms = [value] + [value * factor for factor in factors]
            for pair in range(3):
                both = jnp.concatenate(terms[2 * pair : 2 * pair + 2], 0)
                high = both.astype(BF)
                part = pl.ds((10 + 3 * v + pair) * 16, 16)
                fh_ref[t, part] = high
                fl_ref[t, part] = (both - high.astype(F32)).astype(BF)
    return jnp.concatenate(parts, 1)


def weigh_block(right, blk, m_ref, left, w_ref):
    nodes = m_ref.shape[1]
    start = pl.multiple_of(blk * 8, 8)
    power = lax.dot_general(left[:, :48], right, (((1,), (0,)), ((), ())), preferred_element_type=F32)
    for t in range(8):
        w_high, w_low = split2(jnp.exp2(power[:, t * LANES : (t + 1) * LANES]) * m_ref[start + t])
        w_ref[t, 0:nodes] = w_high
        w_ref[t, nodes:] = w_low


def add_block(fh_ref, fl_ref, w_ref, acc_ref):
    nodes = acc_ref.shape[0]
    def wide(ref, rows):
        return jnp.concatenate([ref[t, 0:rows] for t in range(8)], 1)

    first = lax.dot_general(wide(w_ref, 2 * nodes), wide(fh_ref, 256), NT_DIMS, preferred_element_type=F32)
    second = lax.dot_general(wide(w_ref, nodes), wide(fl_ref, 256), NT_DIMS, preferred_element_type=F32)
    acc_ref[...] += first[:nodes] + first[nodes:] + second


def fit_nodes(acc_ref, frame, out_ref):
    nodes = acc_ref.shape[0]
    columns = acc_ref[...].T
    ex, ey, qx, qy, qz = (jnp.broadcast_to(2.0 * part, (8, nodes)) for part in frame)
    sums = [columns[8 * i : 8 * i + 8, :] for i in range(32)]
    del sums[GROUPS]
    s1, sx, sy, sz, sc, ss, sxx, sxy, sxz, syy, syz, sxc, syc, szc, sxs, sys_, szs, scc, scs = sums[:GROUPS]
    szz = s1 - sxx - syy
    normal = {
        (0, 0): s1,
        (0, 1): ex * sx + ey * sy,
        (0, 2): qx * sx + qy * sy + qz * sz,
        (0, 3): sc,
        (0, 4): ss,
        (1, 1): ex * ex * sxx + 2.0 * ex * ey * sxy + ey * ey * syy,
        (1, 2): ex * qx * sxx + (ex * qy + ey * qx) * sxy + ey * qy * syy + ex * qz * sxz + ey * qz * syz,
        (1, 3): ex * sxc + ey * syc,
        (1, 4): ex * sxs + ey * sys_,
        (2, 2): qx * qx * sxx + qy * qy * syy + qz * qz * szz + 2.0 * (qx * qy * sxy + qx * qz * sxz + qy * qz * syz),
        (2, 3): qx * sxc + qy * syc + qz * szc,
        (2, 4): qx * sxs + qy * sys_ + qz * szs,
        (3, 3): scc,
        (3, 4): scs,
        (4, 4): s1 - scc,
    }
    lower = {}
    inverse = []
    for column in range(5):
        diagonal = normal[column, column] + 1.0
        for inner in range(column):
            diagonal = diagonal - lower[column, inner] * lower[column, inner]
        inverse.append(1.0 / jnp.sqrt(diagonal))
        for target in range(column + 1, 5):
            element = normal[column, target]
            for inner in range(column):
                element = element - lower[target, inner] * lower[column, inner]
            lower[target, column] = element * inverse[column]
    for v in range(2):
        m1, mx, my, mz, mc, ms = sums[GROUPS + 6 * v : GROUPS + 6 * v + 6]
        moments = [m1, ex * mx + ey * my, qx * mx + qy * my + qz * mz, mc, ms]
        forward = []
        for target in range(5):
            residue = moments[target]
            for inner in range(target):
                residue = residue - lower[target, inner] * forward[inner]
            forward.append(residue * inverse[target])
        coeffs = [None] * 5
        for target in reversed(range(5)):
            residue = forward[target]
            for inner in range(target + 1, 5):
                residue = residue - lower[inner, target] * coeffs[inner]
            coeffs[target] = residue * inverse[target]
        out_ref[v] = coeffs[0] + coeffs[3] * math.cos(MONTH_ANGLE) + coeffs[4] * math.sin(MONTH_ANGLE)


def node_frame(longitude, latitude):
    sin_lat, cos_lat = jnp.sin(latitude), jnp.cos(latitude)
    sin_lon, cos_lon = jnp.sin(longitude), jnp.cos(longitude)
    point = (cos_lat * cos_lon, cos_lat * sin_lon, sin_lat)
    frame = (-sin_lon, cos_lon, -sin_lat * cos_lon, -sin_lat * sin_lon, cos_lat)
    return point, frame


def dense_rows(ref, row):
    return jnp.concatenate([ref[row : row + 1, m * LANES : (m + 1) * LANES] for m in range(ref.shape[1] // LANES)], 0)


def profile_meta(place_ref, depth_ref):
    longitude, latitude, day_angle = (dense_rows(place_ref, row) for row in range(3))
    cos_lat = jnp.cos(latitude)
    rows = [
        cos_lat * jnp.cos(longitude),
        cos_lat * jnp.sin(longitude),
        jnp.sin(latitude),
        jnp.cos(day_angle),
        jnp.sin(day_angle),
        dense_rows(depth_ref, 0).astype(F32),
        jnp.ones_like(cos_lat),
        jnp.zeros_like(cos_lat),
    ]
    return jnp.swapaxes(jnp.stack(rows, 0), 0, 1)


def compute(nodes, level_base, early, start, before_count, before_pair, left, ext_ref, hi_ref, lo_ref, m_ref, work):
    tmp_a, tmp_b, gh_a, gl_a, gh_b, gl_b, fh_a, fl_a, w_a, fh_b, fl_b, w_b, acc_ref = work
    acc_ref[...] = jnp.zeros_like(acc_ref)
    count_nodes(0, hi_ref, lo_ref, tmp_a, None, None)
    last = nodes // 16 - 1

    def count_pair(step, carry):
        count_nodes(2 * step + 1, hi_ref, lo_ref, tmp_b, tmp_a, m_ref)
        count_nodes(2 * step + 2, hi_ref, lo_ref, tmp_a, tmp_b, m_ref)
        return carry

    def count_step(step, carry):
        before_count(step)
        return count_pair(step, carry)

    lax.fori_loop(0, early, count_pair, 0)
    start()
    lax.fori_loop(early, last, count_step, 0)
    before_count(last)
    count_nodes(2 * last + 1, hi_ref, lo_ref, tmp_b, tmp_a, m_ref)
    place_counts(2 * last + 1, tmp_b, m_ref, 0, m_ref.shape[0])

    def build(blk, gh_ref, gl_ref, fh_ref, fl_ref, w_ref):
        right = build_block(blk, level_base, ext_ref, gh_ref, gl_ref, fh_ref, fl_ref)
        weigh_block(right, blk, m_ref, left, w_ref)

    set_a = (gh_a, gl_a, fh_a, fl_a, w_a)
    set_b = (gh_b, gl_b, fh_b, fl_b, w_b)
    index = before_pair(0)
    build(2 * index, *set_a)

    def pair_step(pair, index):
        following = before_pair(pair + 1)
        build(2 * index + 1, *set_b)
        add_block(fh_a, fl_a, w_a, acc_ref)
        build(2 * following, *set_a)
        add_block(fh_b, fl_b, w_b, acc_ref)
        return following

    pairs = ext_ref.shape[0] // 16
    index = lax.fori_loop(0, pairs - 1, pair_step, index)
    build(2 * index + 1, *set_b)
    add_block(fh_a, fl_a, w_a, acc_ref)
    add_block(fh_b, fl_b, w_b, acc_ref)


def work_buffers(nodes):
    tile = pltpu.VMEM((8, 192, LANES), F32)
    dense = pltpu.VMEM((GROUPS - 1, 8, LANES), F32)
    wide = pltpu.VMEM((8, 256, LANES), BF)
    return (tile, tile) + (dense,) * 4 + (wide,) * 6 + (pltpu.VMEM((nodes, 256), F32),)


def full_kernel(
    values_ref, place_ref, depth_ref, node_ref, nb_ref, cnt_ref, out_ref,
    meta_ref, sib_values_ref, sib_meta_ref, own_ref, halo_ref, ext_ref,
    hi_ref, lo_ref, m_ref, work,
    send_own, send_halo, recv, pass_send, sib_send, sib_recv,
):
    x = lax.axis_index("band")
    tile = lax.axis_index("tile")
    core = lax.rem(tile, 2)
    chip = lax.div(tile, 2)
    z, y = lax.div(chip, 4), lax.rem(chip, 4)
    sibling = {"tile": tile + 1 - 2 * core}
    mine = chip_slot(x, z, y)
    phase = lax.rem(x + z + y, 4)
    nodes = nb_ref.shape[0]

    def partner(index):
        dx, dy = lax.bitwise_and(lax.shift_right_logical(index, 2), 3), lax.bitwise_and(index, 3)
        dz = lax.shift_right_logical(index, 4) + 8 - dx - dy
        other_x, other_z, other_y = lax.bitwise_and(x + dx, 3), lax.bitwise_and(z + dz, 3), lax.bitwise_and(y + dy, 3)
        pair = other_z * 4 + other_y
        return other_x * 16 + pair, {"band": other_x, "tile": 2 * pair + core}

    barrier = pltpu.get_barrier_semaphore()

    def greet(index, carry):
        _, device = partner(index)
        pl.semaphore_signal(barrier, inc=1, device_id=device, device_id_type=MESH)
        return carry

    lax.fori_loop(1, 64, greet, 0)
    pl.semaphore_signal(barrier, inc=1, device_id=sibling, device_id_type=MESH)

    meta_ref[...] = profile_meta(place_ref, depth_ref)
    for b in range(4):
        for m in range(16):
            for v in range(2):
                own_ref[b * 16 + m, 8 * v : 8 * v + 8, :] = values_ref[v, 8 * b : 8 * b + 8, m * LANES : (m + 1) * LANES]
            own_ref[b * 16 + m, 16:24, :] = meta_ref[m]
    point, frame = node_frame(node_ref[0:1, :], node_ref[1:2, :])
    packed = jnp.concatenate(list(point) + [cnt_ref[...].astype(F32)] + [jnp.zeros((124, nodes), F32)], 0)
    columns = packed.T
    left = node_left(columns[:, 0:1], columns[:, 1:2], columns[:, 2:3])
    list_rows(core, nb_ref, columns[:, 3:4], hi_ref, lo_ref)

    sib_copies = [
        pltpu.make_async_remote_copy(values_ref, sib_values_ref, sib_send.at[0], sib_recv.at[0], device_id=sibling, device_id_type=MESH),
        pltpu.make_async_remote_copy(meta_ref, sib_meta_ref, sib_send.at[1], sib_recv.at[1], device_id=sibling, device_id_type=MESH),
    ]

    def send(buffer, base, send_sem):
        def step(index, carry):
            unit, device = partner(index)
            pltpu.make_async_remote_copy(
                buffer.at[unit], ext_ref.at[16 * base + mine], send_sem, recv.at[base + phase], device_id=device, device_id_type=MESH
            ).start()
            return carry

        lax.fori_loop(1, 64, step, 0)

    def keep(buffer, base):
        return pltpu.make_async_copy(buffer.at[x * 16 + chip], ext_ref.at[16 * base + mine], recv.at[base + phase])

    def group(index):
        return ext_ref.at[pl.ds(pl.multiple_of(index * 16, 16), 16)]

    def wait_group(index):
        pltpu.make_async_copy(group(index), group(index), recv.at[index]).wait()

    def start():
        pl.semaphore_wait(barrier, 64)
        for copy in sib_copies:
            copy.start()
        keep(own_ref, 0).start()
        send(own_ref, 0, send_own)

    def send_halos():
        for copy in sib_copies:
            copy.wait_recv()
        from_own = lax.shift_right_logical(lax.broadcasted_iota(jnp.int32, (8, LANES), 1), 6) == core

        def step(m, carry):
            other = lax.rem(m + 15 + 2 * core, 16)
            cols = pl.ds(pl.multiple_of(other * LANES, LANES), LANES)
            meta = jnp.where(from_own, pltpu.roll(meta_ref[other], 64, 1), sib_meta_ref[other])
            for b in range(4):
                unit = b * 16 + m
                for v in range(2):
                    mine_rows = values_ref[v, 8 * b : 8 * b + 8, cols]
                    their_rows = sib_values_ref[v, 8 * b : 8 * b + 8, cols]
                    halo_ref[unit, 8 * v : 8 * v + 8, :] = jnp.where(from_own, pltpu.roll(mine_rows, 64, 1), their_rows)
                halo_ref[unit, 16:24, :] = meta
            return carry

        lax.fori_loop(0, 16, step, 0)
        keep(halo_ref, 8).start()
        send(halo_ref, 8, send_halo)

    def pass_copy(k):
        return pltpu.make_async_remote_copy(
            group(k), group(4 + k), pass_send.at[k], recv.at[4 + k], device_id=sibling, device_id_type=MESH
        )

    def before_count(step):
        pl.when(step == EARLY + 1)(send_halos)

    def before_pair(pair):
        k = lax.bitwise_and(phase + 4 - pair, 3)
        index = pair - lax.bitwise_and(pair, 3) + k
        wait_group(index)
        pl.when(pair < 4)(lambda: pass_copy(k).start())
        return index

    compute(nodes, x * 8, EARLY, start, before_count, before_pair, left, ext_ref, hi_ref, lo_ref, m_ref, work)
    fit_nodes(work[-1], frame, out_ref)
    for buffer, send_sem in ((own_ref, send_own), (halo_ref, send_halo)):
        view = buffer.at[pl.ds(0, 63)]
        pltpu.make_async_copy(view, view, send_sem).wait()
    for k in range(4):
        pass_copy(k).wait_send()
    for copy in sib_copies:
        copy.wait_send()


def body(obs_values, obs_place, obs_depth, node_place, neighbours, counts):
    nodes, fan = neighbours.shape
    vmem = pl.BlockSpec(memory_space=pltpu.VMEM)
    dma = pltpu.SemaphoreType.DMA
    return pl.pallas_call(
        full_kernel,
        out_shape=jax.ShapeDtypeStruct((2, 8, nodes), F32),
        in_specs=[vmem] * 6,
        out_specs=vmem,
        scratch_shapes=[
            pltpu.VMEM((16, 8, LANES), F32),
            pltpu.VMEM(obs_values.shape, F32),
            pltpu.VMEM((16, 8, LANES), F32),
            pltpu.VMEM((64, 24, LANES), F32),
            pltpu.VMEM((64, 24, LANES), F32),
            pltpu.VMEM((192, 24, LANES), F32),
            pltpu.VMEM((nodes, fan), jnp.int32),
            pltpu.VMEM((nodes, fan), jnp.int32),
            pltpu.VMEM((192, nodes, LANES), F32),
            work_buffers(nodes),
            dma,
            dma,
            dma((12,)),
            dma((4,)),
            dma((2,)),
            dma((2,)),
        ],
        compiler_params=pltpu.CompilerParams(vmem_limit_bytes=VMEM_LIMIT, collective_id=0, has_side_effects=True),
    )(obs_values, obs_place, obs_depth.reshape(1, -1), node_place, neighbours, counts.reshape(1, nodes))


def solution(mesh):
    return jax.shard_map(
        body,
        mesh=mesh,
        in_specs=(
            P(None, None, ("band", "tile")),
            P(None, ("band", "tile")),
            P(("band", "tile")),
            P(None, "tile"),
            P("tile", None),
            P("tile"),
        ),
        out_specs=P(None, "band", "tile"),
        check_vma=False,
    )
```

```python
import math

import jax
import jax.numpy as jnp
from jax import lax
from jax.experimental import pallas as pl
from jax.experimental.pallas import tpu as pltpu
from jax.sharding import PartitionSpec as P

MONTH_ANGLE = -11.0 * math.pi / 12.0
BF = jnp.bfloat16
F32 = jnp.float32
E4 = jnp.float8_e4m3fn
I8 = jnp.int8
NT_DIMS = (((1,), (1,)), ((), ()))
LANES = 128
MESH = pl.DeviceIdType.MESH
GROUPS = 19
EARLY = 1
ROWS = 21
VMEM_LIMIT = 60 * 2**20


def list_rows(core, nb_ref, cnt_col, hi_ref, lo_ref):
    nb = nb_ref[...]
    valid = lax.broadcasted_iota(jnp.int32, nb.shape, 1).astype(F32) < cnt_col
    segment = lax.shift_right_logical(nb, 13)
    chip = lax.bitwise_and(lax.shift_right_logical(nb, 7), 63)
    source_core = lax.bitwise_and(lax.shift_right_logical(nb, 6), 1)
    slot = chip_slot(lax.shift_right_logical(chip, 4), lax.bitwise_and(lax.shift_right_logical(chip, 2), 3), lax.bitwise_and(chip, 3))
    is_halo = segment == 2 * core
    half = segment - 1 + core
    hi = slot + jnp.where(is_halo, 64, jnp.where(source_core == core, -64, 0))
    lo = jnp.where(is_halo, lax.bitwise_and(nb, 127), lax.bitwise_and(nb, 63) + 64 * half)
    hi_ref[...] = jnp.where(valid, hi, -128)
    lo_ref[...] = lo


def chip_slot(x, z, y):
    return lax.bitwise_and(x + z + y, 3) * 16 + x * 4 + y


def count_nodes(step, hi_ref, lo_ref, tmp_ref, last_ref, m_ref):
    fan = hi_ref.shape[1]
    tiles = tmp_ref.shape[1]
    hi_ids = (lax.broadcasted_iota(jnp.int32, (tiles, fan), 0) - 64).astype(I8)
    lo_ids = lax.broadcasted_iota(jnp.int32, (LANES, fan), 0).astype(I8)
    one, zero = jnp.ones((), E4), jnp.zeros((), E4)
    for i in range(8):
        n = step * 8 + i
        hi = jnp.broadcast_to(hi_ref[pl.ds(n, 1), :], (32, fan)).astype(I8)
        lo = jnp.broadcast_to(lo_ref[pl.ds(n, 1), :], (32, fan)).astype(I8)
        hot_hi = jnp.where(hi_ids == jnp.concatenate([hi] * (tiles // 32), 0), one, zero)
        hot_lo = jnp.where(lo_ids == jnp.concatenate([lo] * (LANES // 32), 0), one, zero)
        tmp_ref[i] = lax.dot_general(hot_hi, hot_lo, NT_DIMS, preferred_element_type=F32)
        if last_ref is not None:
            place_counts(step - 1, last_ref, m_ref, i * tiles // 8, (i + 1) * tiles // 8)


def place_counts(step, tmp_ref, m_ref, first, stop):
    m_ref[first:stop, pl.ds(pl.multiple_of(step * 8, 8), 8), :] = jnp.swapaxes(tmp_ref[:, first:stop, :], 0, 1)


def split2(x):
    high = x.astype(BF)
    return high, (x - high.astype(F32)).astype(BF)


def split3(x):
    high = x.astype(BF)
    rest = x - high.astype(F32)
    mid = rest.astype(BF)
    return high, mid, (rest - mid.astype(F32)).astype(BF)


def node_left(node_x, node_y, node_z):
    scale = 8.0 * math.log2(math.e)
    col = lax.broadcasted_iota(jnp.int32, (node_x.shape[0], LANES), 1)
    row = lax.bitwise_and(col, 7)
    vals = jnp.where(
        row == 0,
        node_x * scale,
        jnp.where(row == 1, node_y * scale, jnp.where(row == 2, node_z * scale, jnp.where(row == 3, -scale, 0.0))),
    )
    high, mid, low = split3(vals)
    block = lax.shift_right_logical(col, 3)
    high, mid, low = high.astype(F32), mid.astype(F32), low.astype(F32)
    part = jnp.where(
        (block == 0) | (block == 3) | (block == 5),
        high,
        jnp.where((block == 1) | (block == 4), mid, jnp.where(block == 2, low, 0.0)),
    )
    return part.astype(BF)


def meta_features(meta):
    dense = jnp.swapaxes(meta, 0, 1)
    y, z, c, s = (dense[i] for i in range(4))
    x = jnp.sqrt(jnp.maximum(1.0 - y * y - z * z, 0.0))
    one, zero = jnp.ones_like(x), jnp.zeros_like(x)
    rows = jnp.swapaxes(jnp.stack([x, y, z, one, c, s, zero, zero], 0), 0, 1)
    products = [x, y, z, c, s, x * x, x * y, x * z, y * y, y * z, x * c, y * c, z * c, x * s, y * s, z * s, c * c, c * s]
    return products, rows


def build_block(blk, level_base, ext_ref, gh_ref, gl_ref, fh_ref, fl_ref):
    start = pl.multiple_of(blk * 8, 8)
    meta = ext_ref[pl.ds(start, 8), 16:24, :]
    products, features = meta_features(meta)
    for t in range(8):
        gh_ref[GROUPS - 1 + t] = features[t]
    for index, prod in enumerate(products):
        high = prod.astype(BF).astype(F32)
        gh_ref[index] = high
        gl_ref[index] = prod - high
    level = (lax.broadcasted_iota(jnp.int32, (8, LANES), 0) + level_base).astype(F32)
    zero, one = jnp.zeros((8, LANES), F32), jnp.ones((8, LANES), F32)
    parts = []
    for t in range(8):
        rows = ext_ref[start + t]
        depth = jnp.broadcast_to(rows[20:21], (8, LANES))
        inside = level < depth
        hold = jnp.where(inside, one, zero)
        high, mid, low = split3(features[t])
        high, mid, low = high.astype(F32), mid.astype(F32), low.astype(F32)
        parts.append(jnp.concatenate([high, high, high, mid, mid, low], 0).astype(BF))
        for g_ref, f_ref, first in ((gh_ref, fh_ref, hold), (gl_ref, fl_ref, zero)):
            terms = [jnp.where(inside, jnp.broadcast_to(g_ref[i, t : t + 1, :], (8, LANES)), zero) for i in range(GROUPS - 1)]
            terms = [first] + terms + [zero]
            for pair in range(10):
                f_ref[t, pl.ds(pair * 16, 16)] = jnp.concatenate(terms[2 * pair : 2 * pair + 2], 0).astype(BF)
        factors = [jnp.broadcast_to(gh_ref[GROUPS - 1 + t, i : i + 1, :], (8, LANES)) for i in (0, 1, 2, 4, 5)]
        for v in range(2):
            value = jnp.where(inside, rows[8 * v : 8 * v + 8], zero)
            terms = [value] + [value * factor for factor in factors]
            for pair in range(3):
                both = jnp.concatenate(terms[2 * pair : 2 * pair + 2], 0)
                high = both.astype(BF)
                part = pl.ds((10 + 3 * v + pair) * 16, 16)
                fh_ref[t, part] = high
                fl_ref[t, part] = (both - high.astype(F32)).astype(BF)
    return jnp.concatenate(parts, 1)


def weigh_block(right, blk, m_ref, left, w_ref):
    nodes = m_ref.shape[1]
    start = pl.multiple_of(blk * 8, 8)
    power = lax.dot_general(left[:, :48], right, (((1,), (0,)), ((), ())), preferred_element_type=F32)
    for t in range(8):
        w_high, w_low = split2(jnp.exp2(power[:, t * LANES : (t + 1) * LANES]) * m_ref[start + t])
        w_ref[t, 0:nodes] = w_high
        w_ref[t, nodes:] = w_low


def add_block(fh_ref, fl_ref, w_ref, acc_ref):
    nodes = acc_ref.shape[0]
    def wide(ref, rows):
        return jnp.concatenate([ref[t, 0:rows] for t in range(8)], 1)

    first = lax.dot_general(wide(w_ref, 2 * nodes), wide(fh_ref, 256), NT_DIMS, preferred_element_type=F32)
    second = lax.dot_general(wide(w_ref, nodes), wide(fl_ref, 256), NT_DIMS, preferred_element_type=F32)
    acc_ref[...] += first[:nodes] + first[nodes:] + second


def fit_nodes(acc_ref, frame, out_ref):
    nodes = acc_ref.shape[0]
    columns = acc_ref[...].T
    ex, ey, qx, qy, qz = (jnp.broadcast_to(2.0 * part, (8, nodes)) for part in frame)
    sums = [columns[8 * i : 8 * i + 8, :] for i in range(32)]
    del sums[GROUPS]
    s1, sx, sy, sz, sc, ss, sxx, sxy, sxz, syy, syz, sxc, syc, szc, sxs, sys_, szs, scc, scs = sums[:GROUPS]
    szz = s1 - sxx - syy
    normal = {
        (0, 0): s1,
        (0, 1): ex * sx + ey * sy,
        (0, 2): qx * sx + qy * sy + qz * sz,
        (0, 3): sc,
        (0, 4): ss,
        (1, 1): ex * ex * sxx + 2.0 * ex * ey * sxy + ey * ey * syy,
        (1, 2): ex * qx * sxx + (ex * qy + ey * qx) * sxy + ey * qy * syy + ex * qz * sxz + ey * qz * syz,
        (1, 3): ex * sxc + ey * syc,
        (1, 4): ex * sxs + ey * sys_,
        (2, 2): qx * qx * sxx + qy * qy * syy + qz * qz * szz + 2.0 * (qx * qy * sxy + qx * qz * sxz + qy * qz * syz),
        (2, 3): qx * sxc + qy * syc + qz * szc,
        (2, 4): qx * sxs + qy * sys_ + qz * szs,
        (3, 3): scc,
        (3, 4): scs,
        (4, 4): s1 - scc,
    }
    lower = {}
    inverse = []
    for column in range(5):
        diagonal = normal[column, column] + 1.0
        for inner in range(column):
            diagonal = diagonal - lower[column, inner] * lower[column, inner]
        inverse.append(1.0 / jnp.sqrt(diagonal))
        for target in range(column + 1, 5):
            element = normal[column, target]
            for inner in range(column):
                element = element - lower[target, inner] * lower[column, inner]
            lower[target, column] = element * inverse[column]
    for v in range(2):
        m1, mx, my, mz, mc, ms = sums[GROUPS + 6 * v : GROUPS + 6 * v + 6]
        moments = [m1, ex * mx + ey * my, qx * mx + qy * my + qz * mz, mc, ms]
        forward = []
        for target in range(5):
            residue = moments[target]
            for inner in range(target):
                residue = residue - lower[target, inner] * forward[inner]
            forward.append(residue * inverse[target])
        coeffs = [None] * 5
        for target in reversed(range(5)):
            residue = forward[target]
            for inner in range(target + 1, 5):
                residue = residue - lower[inner, target] * coeffs[inner]
            coeffs[target] = residue * inverse[target]
        out_ref[v] = coeffs[0] + coeffs[3] * math.cos(MONTH_ANGLE) + coeffs[4] * math.sin(MONTH_ANGLE)


def node_frame(longitude, latitude):
    sin_lat, cos_lat = jnp.sin(latitude), jnp.cos(latitude)
    sin_lon, cos_lon = jnp.sin(longitude), jnp.cos(longitude)
    point = (cos_lat * cos_lon, cos_lat * sin_lon, sin_lat)
    frame = (-sin_lon, cos_lon, -sin_lat * cos_lon, -sin_lat * sin_lon, cos_lat)
    return point, frame


def dense_rows(ref, row):
    return jnp.concatenate([ref[row : row + 1, m * LANES : (m + 1) * LANES] for m in range(ref.shape[1] // LANES)], 0)


def profile_meta(place_ref, depth_ref):
    longitude, latitude, day_angle = (dense_rows(place_ref, row) for row in range(3))
    pair = lax.broadcasted_iota(jnp.int32, longitude.shape, 0).astype(F32)
    longitude = longitude - (pair * (math.pi / 8) + (math.pi / 16 - math.pi))
    cos_lat = jnp.cos(latitude)
    rows = [
        cos_lat * jnp.sin(longitude),
        jnp.sin(latitude),
        jnp.cos(day_angle),
        jnp.sin(day_angle),
        dense_rows(depth_ref, 0).astype(F32),
        cos_lat * jnp.cos(longitude),
        jnp.zeros_like(cos_lat),
        jnp.zeros_like(cos_lat),
    ]
    return jnp.swapaxes(jnp.stack(rows, 0), 0, 1)


def compute(nodes, level_base, early, start, before_count, before_pair, left, ext_ref, hi_ref, lo_ref, m_ref, work):
    tmp_a, tmp_b, gh_a, gl_a, gh_b, gl_b, fh_a, fl_a, w_a, fh_b, fl_b, w_b, acc_ref = work
    acc_ref[...] = jnp.zeros_like(acc_ref)
    count_nodes(0, hi_ref, lo_ref, tmp_a, None, None)
    last = nodes // 16 - 1

    def count_pair(step, carry):
        count_nodes(2 * step + 1, hi_ref, lo_ref, tmp_b, tmp_a, m_ref)
        count_nodes(2 * step + 2, hi_ref, lo_ref, tmp_a, tmp_b, m_ref)
        return carry

    def count_step(step, carry):
        before_count(step)
        return count_pair(step, carry)

    lax.fori_loop(0, early, count_pair, 0)
    start()
    lax.fori_loop(early, last, count_step, 0)
    before_count(last)
    count_nodes(2 * last + 1, hi_ref, lo_ref, tmp_b, tmp_a, m_ref)
    place_counts(2 * last + 1, tmp_b, m_ref, 0, m_ref.shape[0])

    def build(blk, gh_ref, gl_ref, fh_ref, fl_ref, w_ref):
        right = build_block(blk, level_base, ext_ref, gh_ref, gl_ref, fh_ref, fl_ref)
        weigh_block(right, blk, m_ref, left, w_ref)

    set_a = (gh_a, gl_a, fh_a, fl_a, w_a)
    set_b = (gh_b, gl_b, fh_b, fl_b, w_b)
    index = before_pair(0)
    build(2 * index, *set_a)

    def pair_step(pair, index):
        following = before_pair(pair + 1)
        build(2 * index + 1, *set_b)
        add_block(fh_a, fl_a, w_a, acc_ref)
        build(2 * following, *set_a)
        add_block(fh_b, fl_b, w_b, acc_ref)
        return following

    pairs = ext_ref.shape[0] // 16
    index = lax.fori_loop(0, pairs - 1, pair_step, index)
    build(2 * index + 1, *set_b)
    add_block(fh_a, fl_a, w_a, acc_ref)
    add_block(fh_b, fl_b, w_b, acc_ref)


def work_buffers(nodes):
    tile = pltpu.VMEM((8, 192, LANES), F32)
    dense = pltpu.VMEM((GROUPS + 7, 8, LANES), F32)
    wide = pltpu.VMEM((8, 256, LANES), BF)
    return (tile, tile) + (dense,) * 4 + (wide,) * 6 + (pltpu.VMEM((nodes, 256), F32),)


def full_kernel(
    values_ref, place_ref, depth_ref, node_ref, nb_ref, cnt_ref, out_ref,
    meta_ref, sib_values_ref, sib_meta_ref, own_ref, halo_ref, ext_ref,
    hi_ref, lo_ref, m_ref, work,
    send_own, send_halo, recv, pass_send, sib_send, sib_recv,
):
    x = lax.axis_index("band")
    tile = lax.axis_index("tile")
    core = lax.rem(tile, 2)
    chip = lax.div(tile, 2)
    z, y = lax.div(chip, 4), lax.rem(chip, 4)
    sibling = {"tile": tile + 1 - 2 * core}
    mine = chip_slot(x, z, y)
    phase = lax.rem(x + z + y, 4)
    nodes = nb_ref.shape[0]

    def partner(index):
        dx, dy = lax.bitwise_and(lax.shift_right_logical(index, 2), 3), lax.bitwise_and(index, 3)
        dz = lax.shift_right_logical(index, 4) + 8 - dx - dy
        other_x, other_z, other_y = lax.bitwise_and(x + dx, 3), lax.bitwise_and(z + dz, 3), lax.bitwise_and(y + dy, 3)
        pair = other_z * 4 + other_y
        return other_x * 16 + pair, {"band": other_x, "tile": 2 * pair + core}

    barrier = pltpu.get_barrier_semaphore()

    def greet(index, carry):
        _, device = partner(index)
        pl.semaphore_signal(barrier, inc=1, device_id=device, device_id_type=MESH)
        return carry

    lax.fori_loop(1, 64, greet, 0)
    pl.semaphore_signal(barrier, inc=1, device_id=sibling, device_id_type=MESH)

    meta_ref[...] = profile_meta(place_ref, depth_ref)
    for b in range(4):
        for m in range(16):
            for v in range(2):
                own_ref[b * 16 + m, 8 * v : 8 * v + 8, :] = values_ref[v, 8 * b : 8 * b + 8, m * LANES : (m + 1) * LANES]
            own_ref[b * 16 + m, 16:24, :] = meta_ref[m]
    middle = jnp.full((1, nodes), chip, jnp.int32).astype(F32) * (math.pi / 8) + (math.pi / 16 - math.pi)
    point, frame = node_frame(node_ref[0:1, :] - middle, node_ref[1:2, :])
    packed = jnp.concatenate(list(point) + [cnt_ref[...].astype(F32)] + [jnp.zeros((124, nodes), F32)], 0)
    columns = packed.T
    left = node_left(columns[:, 0:1], columns[:, 1:2], columns[:, 2:3])
    list_rows(core, nb_ref, columns[:, 3:4], hi_ref, lo_ref)

    sib_copies = [
        pltpu.make_async_remote_copy(values_ref, sib_values_ref, sib_send.at[0], sib_recv.at[0], device_id=sibling, device_id_type=MESH),
        pltpu.make_async_remote_copy(meta_ref, sib_meta_ref, sib_send.at[1], sib_recv.at[1], device_id=sibling, device_id_type=MESH),
    ]

    def send(buffer, base, send_sem):
        def step(index, carry):
            unit, device = partner(index)
            pltpu.make_async_remote_copy(
                buffer.at[unit, pl.ds(0, ROWS)], ext_ref.at[16 * base + mine, pl.ds(0, ROWS)], send_sem, recv.at[base + phase], device_id=device, device_id_type=MESH
            ).start()
            return carry

        lax.fori_loop(1, 64, step, 0)

    def keep(buffer, base):
        return pltpu.make_async_copy(buffer.at[x * 16 + chip, pl.ds(0, ROWS)], ext_ref.at[16 * base + mine, pl.ds(0, ROWS)], recv.at[base + phase])

    def group(index):
        return ext_ref.at[pl.ds(pl.multiple_of(index * 16, 16), 16), pl.ds(0, ROWS)]

    def wait_group(index):
        pltpu.make_async_copy(group(index), group(index), recv.at[index]).wait()

    def start():
        pl.semaphore_wait(barrier, 64)
        for copy in sib_copies:
            copy.start()
        keep(own_ref, 0).start()
        send(own_ref, 0, send_own)

    def send_halos():
        for copy in sib_copies:
            copy.wait_recv()
        turn = jnp.full((1, LANES), 2 * core - 1, jnp.int32).astype(F32) * math.sin(math.pi / 8)
        first_row = lax.broadcasted_iota(jnp.int32, (8, LANES), 0) == 0
        from_own = lax.shift_right_logical(lax.broadcasted_iota(jnp.int32, (8, LANES), 1), 6) == core

        def step(m, carry):
            other = lax.rem(m + 15 + 2 * core, 16)
            cols = pl.ds(pl.multiple_of(other * LANES, LANES), LANES)
            meta = jnp.where(from_own, pltpu.roll(meta_ref[other], 64, 1), sib_meta_ref[other])
            turned = meta[0:1] * math.cos(math.pi / 8) + meta[5:6] * turn
            meta = jnp.where(first_row, jnp.broadcast_to(turned, (8, LANES)), meta)
            for b in range(4):
                unit = b * 16 + m
                for v in range(2):
                    mine_rows = values_ref[v, 8 * b : 8 * b + 8, cols]
                    their_rows = sib_values_ref[v, 8 * b : 8 * b + 8, cols]
                    halo_ref[unit, 8 * v : 8 * v + 8, :] = jnp.where(from_own, pltpu.roll(mine_rows, 64, 1), their_rows)
                halo_ref[unit, 16:24, :] = meta
            return carry

        lax.fori_loop(0, 16, step, 0)
        keep(halo_ref, 8).start()
        send(halo_ref, 8, send_halo)

    def pass_copy(k):
        return pltpu.make_async_remote_copy(
            group(k), group(4 + k), pass_send.at[k], recv.at[4 + k], device_id=sibling, device_id_type=MESH
        )

    def before_count(step):
        pl.when(step == EARLY + 1)(send_halos)

    def before_pair(pair):
        k = lax.bitwise_and(phase + 4 - pair, 3)
        index = pair - lax.bitwise_and(pair, 3) + k
        wait_group(index)
        pl.when(pair < 4)(lambda: pass_copy(k).start())
        return index

    compute(nodes, x * 8, EARLY, start, before_count, before_pair, left, ext_ref, hi_ref, lo_ref, m_ref, work)
    fit_nodes(work[-1], frame, out_ref)
    for buffer, send_sem in ((own_ref, send_own), (halo_ref, send_halo)):
        view = buffer.at[pl.ds(0, 63), pl.ds(0, ROWS)]
        pltpu.make_async_copy(view, view, send_sem).wait()
    for k in range(4):
        pass_copy(k).wait_send()
    for copy in sib_copies:
        copy.wait_send()


def body(obs_values, obs_place, obs_depth, node_place, neighbours, counts):
    nodes, fan = neighbours.shape
    vmem = pl.BlockSpec(memory_space=pltpu.VMEM)
    dma = pltpu.SemaphoreType.DMA
    return pl.pallas_call(
        full_kernel,
        out_shape=jax.ShapeDtypeStruct((2, 8, nodes), F32),
        in_specs=[vmem] * 6,
        out_specs=vmem,
        scratch_shapes=[
            pltpu.VMEM((16, 8, LANES), F32),
            pltpu.VMEM(obs_values.shape, F32),
            pltpu.VMEM((16, 8, LANES), F32),
            pltpu.VMEM((64, 24, LANES), F32),
            pltpu.VMEM((64, 24, LANES), F32),
            pltpu.VMEM((192, 24, LANES), F32),
            pltpu.VMEM((nodes, fan), jnp.int32),
            pltpu.VMEM((nodes, fan), jnp.int32),
            pltpu.VMEM((192, nodes, LANES), F32),
            work_buffers(nodes),
            dma,
            dma,
            dma((12,)),
            dma((4,)),
            dma((2,)),
            dma((2,)),
        ],
        compiler_params=pltpu.CompilerParams(vmem_limit_bytes=VMEM_LIMIT, collective_id=0, has_side_effects=True),
    )(obs_values, obs_place, obs_depth.reshape(1, -1), node_place, neighbours, counts.reshape(1, nodes))


def solution(mesh):
    return jax.shard_map(
        body,
        mesh=mesh,
        in_specs=(
            P(None, None, ("band", "tile")),
            P(None, ("band", "tile")),
            P(("band", "tile")),
            P(None, "tile"),
            P("tile", None),
            P("tile"),
        ),
        out_specs=P(None, "band", "tile"),
        check_vma=False,
    )
```

```python
import math

import jax
import jax.numpy as jnp
from jax import lax
from jax.experimental import pallas as pl
from jax.experimental.pallas import tpu as pltpu
from jax.sharding import PartitionSpec as P

MONTH_ANGLE = -11.0 * math.pi / 12.0
BF = jnp.bfloat16
F32 = jnp.float32
E4 = jnp.float8_e4m3fn
I8 = jnp.int8
NT_DIMS = (((1,), (1,)), ((), ()))
LANES = 128
MESH = pl.DeviceIdType.MESH
GROUPS = 19
EARLY = 1
ROWS = 21
VMEM_LIMIT = 60 * 2**20


def list_rows(core, nb_ref, cnt_col, hi_ref, lo_ref):
    nb = nb_ref[...]
    valid = lax.broadcasted_iota(jnp.int32, nb.shape, 1).astype(F32) < cnt_col
    segment = lax.shift_right_logical(nb, 13)
    chip = lax.bitwise_and(lax.shift_right_logical(nb, 7), 63)
    source_core = lax.bitwise_and(lax.shift_right_logical(nb, 6), 1)
    slot = chip_slot(lax.shift_right_logical(chip, 4), lax.bitwise_and(lax.shift_right_logical(chip, 2), 3), lax.bitwise_and(chip, 3))
    is_halo = segment == 2 * core
    half = segment - 1 + core
    hi = slot + jnp.where(is_halo, 64, jnp.where(source_core == core, -64, 0))
    lo = jnp.where(is_halo, lax.bitwise_and(nb, 127), lax.bitwise_and(nb, 63) + 64 * half)
    hi_ref[...] = jnp.where(valid, hi, -128)
    lo_ref[...] = lo


def chip_slot(x, z, y):
    return lax.bitwise_and(x + z + y, 3) * 16 + x * 4 + y


def count_nodes(step, hi_ref, lo_ref, tmp_ref, last_ref, m_ref):
    fan = hi_ref.shape[1]
    tiles = tmp_ref.shape[1]
    hi_ids = (lax.broadcasted_iota(jnp.int32, (tiles, fan), 0) - 64).astype(I8)
    lo_ids = lax.broadcasted_iota(jnp.int32, (LANES, fan), 0).astype(I8)
    one, zero = jnp.ones((), E4), jnp.zeros((), E4)
    for i in range(8):
        n = step * 8 + i
        hi = jnp.broadcast_to(hi_ref[pl.ds(n, 1), :], (32, fan)).astype(I8)
        lo = jnp.broadcast_to(lo_ref[pl.ds(n, 1), :], (32, fan)).astype(I8)
        hot_hi = jnp.where(hi_ids == jnp.concatenate([hi] * (tiles // 32), 0), one, zero)
        hot_lo = jnp.where(lo_ids == jnp.concatenate([lo] * (LANES // 32), 0), one, zero)
        tmp_ref[i] = lax.dot_general(hot_hi, hot_lo, NT_DIMS, preferred_element_type=F32)
        if last_ref is not None:
            place_counts(step - 1, last_ref, m_ref, i * tiles // 8, (i + 1) * tiles // 8)


def place_counts(step, tmp_ref, m_ref, first, stop):
    m_ref[first:stop, pl.ds(pl.multiple_of(step * 8, 8), 8), :] = jnp.swapaxes(tmp_ref[:, first:stop, :], 0, 1)


def split2(x):
    high = x.astype(BF)
    return high, (x - high.astype(F32)).astype(BF)


def split3(x):
    high = x.astype(BF)
    rest = x - high.astype(F32)
    mid = rest.astype(BF)
    return high, mid, (rest - mid.astype(F32)).astype(BF)


def node_left(node_x, node_y, node_z):
    scale = 8.0 * math.log2(math.e)
    col = lax.broadcasted_iota(jnp.int32, (node_x.shape[0], LANES), 1)
    row = lax.bitwise_and(col, 7)
    vals = jnp.where(
        row == 0,
        node_x * scale,
        jnp.where(row == 1, node_y * scale, jnp.where(row == 2, node_z * scale, jnp.where(row == 3, -scale, 0.0))),
    )
    high, mid, low = split3(vals)
    block = lax.shift_right_logical(col, 3)
    high, mid, low = high.astype(F32), mid.astype(F32), low.astype(F32)
    part = jnp.where(
        (block == 0) | (block == 3) | (block == 5),
        high,
        jnp.where((block == 1) | (block == 4), mid, jnp.where(block == 2, low, 0.0)),
    )
    return part.astype(BF)


def meta_features(meta):
    dense = jnp.swapaxes(meta, 0, 1)
    y, z, c, s = (dense[i] for i in range(4))
    x = jnp.sqrt(jnp.maximum(1.0 - y * y - z * z, 0.0))
    one, zero = jnp.ones_like(x), jnp.zeros_like(x)
    rows = jnp.swapaxes(jnp.stack([x, y, z, one, c, s, zero, zero], 0), 0, 1)
    products = [x, y, z, c, s, x * x, x * y, x * z, y * y, y * z, x * c, y * c, z * c, x * s, y * s, z * s, c * c, c * s]
    return products, rows


def build_block(blk, level_base, ext_ref, gh_ref, gl_ref, fh_ref, fl_ref):
    start = pl.multiple_of(blk * 8, 8)
    meta = ext_ref[pl.ds(start, 8), 16:24, :]
    products, features = meta_features(meta)
    for t in range(8):
        gh_ref[GROUPS - 1 + t] = features[t]
    for index, prod in enumerate(products):
        high = prod.astype(BF).astype(F32)
        gh_ref[index] = high
        gl_ref[index] = prod - high
    level = (lax.broadcasted_iota(jnp.int32, (8, LANES), 0) + level_base).astype(F32)
    zero, one = jnp.zeros((8, LANES), F32), jnp.ones((8, LANES), F32)
    parts = []
    for t in range(8):
        rows = ext_ref[start + t]
        depth = jnp.broadcast_to(rows[20:21], (8, LANES))
        inside = level < depth
        hold = jnp.where(inside, one, zero)
        high, mid, low = split3(features[t])
        high, mid, low = high.astype(F32), mid.astype(F32), low.astype(F32)
        parts.append(jnp.concatenate([high, high, high, mid, mid, low], 0).astype(BF))
        for g_ref, f_ref, first in ((gh_ref, fh_ref, hold), (gl_ref, fl_ref, zero)):
            terms = [jnp.where(inside, jnp.broadcast_to(g_ref[i, t : t + 1, :], (8, LANES)), zero) for i in range(GROUPS - 1)]
            terms = [first] + terms + [zero]
            for pair in range(10):
                f_ref[t, pl.ds(pair * 16, 16)] = jnp.concatenate(terms[2 * pair : 2 * pair + 2], 0).astype(BF)
        factors = [jnp.broadcast_to(gh_ref[GROUPS - 1 + t, i : i + 1, :], (8, LANES)) for i in (0, 1, 2, 4, 5)]
        for v in range(2):
            value = jnp.where(inside, rows[8 * v : 8 * v + 8], zero)
            terms = [value] + [value * factor for factor in factors]
            for pair in range(3):
                both = jnp.concatenate(terms[2 * pair : 2 * pair + 2], 0)
                high = both.astype(BF)
                part = pl.ds((10 + 3 * v + pair) * 16, 16)
                fh_ref[t, part] = high
                fl_ref[t, part] = (both - high.astype(F32)).astype(BF)
    return jnp.concatenate(parts, 1)


def weigh_block(right, blk, m_ref, left, w_ref):
    nodes = m_ref.shape[1]
    start = pl.multiple_of(blk * 8, 8)
    power = lax.dot_general(left[:, :48], right, (((1,), (0,)), ((), ())), preferred_element_type=F32)
    for t in range(8):
        w_high, w_low = split2(jnp.exp2(power[:, t * LANES : (t + 1) * LANES]) * m_ref[start + t])
        w_ref[t, 0:nodes] = w_high
        w_ref[t, nodes:] = w_low


def add_block(fh_ref, fl_ref, w_ref, acc_ref):
    nodes = acc_ref.shape[0]
    def wide(ref, rows):
        return jnp.concatenate([ref[t, 0:rows] for t in range(8)], 1)

    first = lax.dot_general(wide(w_ref, 2 * nodes), wide(fh_ref, 256), NT_DIMS, preferred_element_type=F32)
    second = lax.dot_general(wide(w_ref, nodes), wide(fl_ref, 256), NT_DIMS, preferred_element_type=F32)
    acc_ref[...] += first[:nodes] + first[nodes:] + second


def fit_nodes(acc_ref, frame, out_ref):
    nodes = acc_ref.shape[0]
    columns = acc_ref[...].T
    ex, ey, qx, qy, qz = (jnp.broadcast_to(2.0 * part, (8, nodes)) for part in frame)
    sums = [columns[8 * i : 8 * i + 8, :] for i in range(32)]
    del sums[GROUPS]
    s1, sx, sy, sz, sc, ss, sxx, sxy, sxz, syy, syz, sxc, syc, szc, sxs, sys_, szs, scc, scs = sums[:GROUPS]
    szz = s1 - sxx - syy
    normal = {
        (0, 0): s1,
        (0, 1): ex * sx + ey * sy,
        (0, 2): qx * sx + qy * sy + qz * sz,
        (0, 3): sc,
        (0, 4): ss,
        (1, 1): ex * ex * sxx + 2.0 * ex * ey * sxy + ey * ey * syy,
        (1, 2): ex * qx * sxx + (ex * qy + ey * qx) * sxy + ey * qy * syy + ex * qz * sxz + ey * qz * syz,
        (1, 3): ex * sxc + ey * syc,
        (1, 4): ex * sxs + ey * sys_,
        (2, 2): qx * qx * sxx + qy * qy * syy + qz * qz * szz + 2.0 * (qx * qy * sxy + qx * qz * sxz + qy * qz * syz),
        (2, 3): qx * sxc + qy * syc + qz * szc,
        (2, 4): qx * sxs + qy * sys_ + qz * szs,
        (3, 3): scc,
        (3, 4): scs,
        (4, 4): s1 - scc,
    }
    lower = {}
    inverse = []
    for column in range(5):
        diagonal = normal[column, column] + 1.0
        for inner in range(column):
            diagonal = diagonal - lower[column, inner] * lower[column, inner]
        inverse.append(1.0 / jnp.sqrt(diagonal))
        for target in range(column + 1, 5):
            element = normal[column, target]
            for inner in range(column):
                element = element - lower[target, inner] * lower[column, inner]
            lower[target, column] = element * inverse[column]
    for v in range(2):
        m1, mx, my, mz, mc, ms = sums[GROUPS + 6 * v : GROUPS + 6 * v + 6]
        moments = [m1, ex * mx + ey * my, qx * mx + qy * my + qz * mz, mc, ms]
        forward = []
        for target in range(5):
            residue = moments[target]
            for inner in range(target):
                residue = residue - lower[target, inner] * forward[inner]
            forward.append(residue * inverse[target])
        coeffs = [None] * 5
        for target in reversed(range(5)):
            residue = forward[target]
            for inner in range(target + 1, 5):
                residue = residue - lower[inner, target] * coeffs[inner]
            coeffs[target] = residue * inverse[target]
        out_ref[v] = coeffs[0] + coeffs[3] * math.cos(MONTH_ANGLE) + coeffs[4] * math.sin(MONTH_ANGLE)


def node_frame(longitude, latitude):
    sin_lat, cos_lat = jnp.sin(latitude), jnp.cos(latitude)
    sin_lon, cos_lon = jnp.sin(longitude), jnp.cos(longitude)
    point = (cos_lat * cos_lon, cos_lat * sin_lon, sin_lat)
    frame = (-sin_lon, cos_lon, -sin_lat * cos_lon, -sin_lat * sin_lon, cos_lat)
    return point, frame


def dense_rows(ref, row):
    return jnp.concatenate([ref[row : row + 1, m * LANES : (m + 1) * LANES] for m in range(ref.shape[1] // LANES)], 0)


def profile_meta(place_ref, depth_ref):
    longitude, latitude, day_angle = (dense_rows(place_ref, row) for row in range(3))
    pair = lax.broadcasted_iota(jnp.int32, longitude.shape, 0).astype(F32)
    longitude = longitude - (pair * (math.pi / 8) + (math.pi / 16 - math.pi))
    cos_lat = jnp.cos(latitude)
    rows = [
        cos_lat * jnp.sin(longitude),
        jnp.sin(latitude),
        jnp.cos(day_angle),
        jnp.sin(day_angle),
        dense_rows(depth_ref, 0).astype(F32),
        cos_lat * jnp.cos(longitude),
        jnp.zeros_like(cos_lat),
        jnp.zeros_like(cos_lat),
    ]
    return jnp.swapaxes(jnp.stack(rows, 0), 0, 1)


def compute(nodes, level_base, early, start, before_count, before_pair, left, ext_ref, hi_ref, lo_ref, m_ref, work):
    tmp_a, tmp_b, gh_a, gl_a, gh_b, gl_b, fh_a, fl_a, w_a, fh_b, fl_b, w_b, acc_ref = work
    acc_ref[...] = jnp.zeros_like(acc_ref)
    count_nodes(0, hi_ref, lo_ref, tmp_a, None, None)

    def count_group(step, odd):
        now, last = (tmp_b, tmp_a) if odd else (tmp_a, tmp_b)
        count_nodes(step, hi_ref, lo_ref, now, last, m_ref)

    def count_four(step, carry):
        for i in range(4):
            count_group(4 * step + 1 + i, i % 2 == 0)
        return carry

    def count_step(step, carry):
        before_count(step)
        return count_four(step, carry)

    rounds = (nodes // 8 - 1) // 4
    lax.fori_loop(0, early, count_four, 0)
    start()
    lax.fori_loop(early, rounds, count_step, 0)
    for step in range(4 * rounds + 1, nodes // 8):
        count_group(step, step % 2 == 1)
    place_counts(nodes // 8 - 1, tmp_b, m_ref, 0, m_ref.shape[0])

    def build(blk, gh_ref, gl_ref, fh_ref, fl_ref, w_ref):
        right = build_block(blk, level_base, ext_ref, gh_ref, gl_ref, fh_ref, fl_ref)
        weigh_block(right, blk, m_ref, left, w_ref)

    set_a = (gh_a, gl_a, fh_a, fl_a, w_a)
    set_b = (gh_b, gl_b, fh_b, fl_b, w_b)
    index = before_pair(0)
    build(2 * index, *set_a)

    def pair_step(pair, index):
        following = before_pair(pair + 1)
        build(2 * index + 1, *set_b)
        add_block(fh_a, fl_a, w_a, acc_ref)
        build(2 * following, *set_a)
        add_block(fh_b, fl_b, w_b, acc_ref)
        return following

    pairs = ext_ref.shape[0] // 16
    index = lax.fori_loop(0, pairs - 1, pair_step, index)
    build(2 * index + 1, *set_b)
    add_block(fh_a, fl_a, w_a, acc_ref)
    add_block(fh_b, fl_b, w_b, acc_ref)


def work_buffers(nodes):
    tile = pltpu.VMEM((8, 192, LANES), F32)
    dense = pltpu.VMEM((GROUPS + 7, 8, LANES), F32)
    wide = pltpu.VMEM((8, 256, LANES), BF)
    return (tile, tile) + (dense,) * 4 + (wide,) * 6 + (pltpu.VMEM((nodes, 256), F32),)


def full_kernel(
    values_ref, place_ref, depth_ref, node_ref, nb_ref, cnt_ref, out_ref,
    meta_ref, sib_values_ref, sib_meta_ref, own_ref, halo_ref, ext_ref,
    hi_ref, lo_ref, m_ref, work,
    send_own, send_halo, recv, pass_send, sib_send, sib_recv,
):
    x = lax.axis_index("band")
    tile = lax.axis_index("tile")
    core = lax.rem(tile, 2)
    chip = lax.div(tile, 2)
    z, y = lax.div(chip, 4), lax.rem(chip, 4)
    sibling = {"tile": tile + 1 - 2 * core}
    mine = chip_slot(x, z, y)
    phase = lax.rem(x + z + y, 4)
    nodes = nb_ref.shape[0]

    def partner(index):
        dx, dy = lax.bitwise_and(lax.shift_right_logical(index, 2), 3), lax.bitwise_and(index, 3)
        dz = lax.shift_right_logical(index, 4) + 8 - dx - dy
        other_x, other_z, other_y = lax.bitwise_and(x + dx, 3), lax.bitwise_and(z + dz, 3), lax.bitwise_and(y + dy, 3)
        pair = other_z * 4 + other_y
        return other_x * 16 + pair, {"band": other_x, "tile": 2 * pair + core}

    barrier = pltpu.get_barrier_semaphore()

    def greet(index, carry):
        _, device = partner(index)
        pl.semaphore_signal(barrier, inc=1, device_id=device, device_id_type=MESH)
        return carry

    lax.fori_loop(1, 64, greet, 0)
    pl.semaphore_signal(barrier, inc=1, device_id=sibling, device_id_type=MESH)

    meta_ref[...] = profile_meta(place_ref, depth_ref)
    for b in range(4):
        for m in range(16):
            for v in range(2):
                own_ref[b * 16 + m, 8 * v : 8 * v + 8, :] = values_ref[v, 8 * b : 8 * b + 8, m * LANES : (m + 1) * LANES]
            own_ref[b * 16 + m, 16:24, :] = meta_ref[m]
    middle = jnp.full((1, nodes), chip, jnp.int32).astype(F32) * (math.pi / 8) + (math.pi / 16 - math.pi)
    point, frame = node_frame(node_ref[0:1, :] - middle, node_ref[1:2, :])
    packed = jnp.concatenate(list(point) + [cnt_ref[...].astype(F32)] + [jnp.zeros((124, nodes), F32)], 0)
    columns = packed.T
    left = node_left(columns[:, 0:1], columns[:, 1:2], columns[:, 2:3])
    list_rows(core, nb_ref, columns[:, 3:4], hi_ref, lo_ref)

    sib_copies = [
        pltpu.make_async_remote_copy(values_ref, sib_values_ref, sib_send.at[0], sib_recv.at[0], device_id=sibling, device_id_type=MESH),
        pltpu.make_async_remote_copy(meta_ref, sib_meta_ref, sib_send.at[1], sib_recv.at[1], device_id=sibling, device_id_type=MESH),
    ]

    def send(buffer, base, send_sem):
        def step(index, carry):
            unit, device = partner(index)
            pltpu.make_async_remote_copy(
                buffer.at[unit, pl.ds(0, ROWS)], ext_ref.at[16 * base + mine, pl.ds(0, ROWS)], send_sem, recv.at[base + phase], device_id=device, device_id_type=MESH
            ).start()
            return carry

        lax.fori_loop(1, 64, step, 0)

    def keep(buffer, base):
        return pltpu.make_async_copy(buffer.at[x * 16 + chip, pl.ds(0, ROWS)], ext_ref.at[16 * base + mine, pl.ds(0, ROWS)], recv.at[base + phase])

    def group(index):
        return ext_ref.at[pl.ds(pl.multiple_of(index * 16, 16), 16), pl.ds(0, ROWS)]

    def wait_group(index):
        pltpu.make_async_copy(group(index), group(index), recv.at[index]).wait()

    def start():
        pl.semaphore_wait(barrier, 64)
        for copy in sib_copies:
            copy.start()
        keep(own_ref, 0).start()
        send(own_ref, 0, send_own)

    def send_halos():
        for copy in sib_copies:
            copy.wait_recv()
        turn = jnp.full((1, LANES), 2 * core - 1, jnp.int32).astype(F32) * math.sin(math.pi / 8)
        first_row = lax.broadcasted_iota(jnp.int32, (8, LANES), 0) == 0
        from_own = lax.shift_right_logical(lax.broadcasted_iota(jnp.int32, (8, LANES), 1), 6) == core

        def step(m, carry):
            other = lax.rem(m + 15 + 2 * core, 16)
            cols = pl.ds(pl.multiple_of(other * LANES, LANES), LANES)
            meta = jnp.where(from_own, pltpu.roll(meta_ref[other], 64, 1), sib_meta_ref[other])
            turned = meta[0:1] * math.cos(math.pi / 8) + meta[5:6] * turn
            meta = jnp.where(first_row, jnp.broadcast_to(turned, (8, LANES)), meta)
            for b in range(4):
                unit = b * 16 + m
                for v in range(2):
                    mine_rows = values_ref[v, 8 * b : 8 * b + 8, cols]
                    their_rows = sib_values_ref[v, 8 * b : 8 * b + 8, cols]
                    halo_ref[unit, 8 * v : 8 * v + 8, :] = jnp.where(from_own, pltpu.roll(mine_rows, 64, 1), their_rows)
                halo_ref[unit, 16:24, :] = meta
            return carry

        lax.fori_loop(0, 16, step, 0)
        keep(halo_ref, 8).start()
        send(halo_ref, 8, send_halo)

    def pass_copy(k):
        return pltpu.make_async_remote_copy(
            group(k), group(4 + k), pass_send.at[k], recv.at[4 + k], device_id=sibling, device_id_type=MESH
        )

    def before_count(step):
        pl.when(step == EARLY + 1)(send_halos)

    def before_pair(pair):
        k = lax.bitwise_and(phase + 4 - pair, 3)
        index = pair - lax.bitwise_and(pair, 3) + k
        wait_group(index)
        pl.when(pair < 4)(lambda: pass_copy(k).start())
        return index

    compute(nodes, x * 8, EARLY, start, before_count, before_pair, left, ext_ref, hi_ref, lo_ref, m_ref, work)
    fit_nodes(work[-1], frame, out_ref)
    for buffer, send_sem in ((own_ref, send_own), (halo_ref, send_halo)):
        view = buffer.at[pl.ds(0, 63), pl.ds(0, ROWS)]
        pltpu.make_async_copy(view, view, send_sem).wait()
    for k in range(4):
        pass_copy(k).wait_send()
    for copy in sib_copies:
        copy.wait_send()


def body(obs_values, obs_place, obs_depth, node_place, neighbours, counts):
    nodes, fan = neighbours.shape
    vmem = pl.BlockSpec(memory_space=pltpu.VMEM)
    dma = pltpu.SemaphoreType.DMA
    return pl.pallas_call(
        full_kernel,
        out_shape=jax.ShapeDtypeStruct((2, 8, nodes), F32),
        in_specs=[vmem] * 6,
        out_specs=vmem,
        scratch_shapes=[
            pltpu.VMEM((16, 8, LANES), F32),
            pltpu.VMEM(obs_values.shape, F32),
            pltpu.VMEM((16, 8, LANES), F32),
            pltpu.VMEM((64, 24, LANES), F32),
            pltpu.VMEM((64, 24, LANES), F32),
            pltpu.VMEM((192, 24, LANES), F32),
            pltpu.VMEM((nodes, fan), jnp.int32),
            pltpu.VMEM((nodes, fan), jnp.int32),
            pltpu.VMEM((192, nodes, LANES), F32),
            work_buffers(nodes),
            dma,
            dma,
            dma((12,)),
            dma((4,)),
            dma((2,)),
            dma((2,)),
        ],
        compiler_params=pltpu.CompilerParams(vmem_limit_bytes=VMEM_LIMIT, collective_id=0, has_side_effects=True),
    )(obs_values, obs_place, obs_depth.reshape(1, -1), node_place, neighbours, counts.reshape(1, nodes))


def solution(mesh):
    return jax.shard_map(
        body,
        mesh=mesh,
        in_specs=(
            P(None, None, ("band", "tile")),
            P(None, ("band", "tile")),
            P(("band", "tile")),
            P(None, "tile"),
            P("tile", None),
            P("tile"),
        ),
        out_specs=P(None, "band", "tile"),
        check_vma=False,
    )
```

```python
import math

import jax
import jax.numpy as jnp
from jax import lax
from jax.experimental import pallas as pl
from jax.experimental.pallas import tpu as pltpu
from jax.sharding import PartitionSpec as P

MONTH_ANGLE = -11.0 * math.pi / 12.0
BF = jnp.bfloat16
F32 = jnp.float32
E4 = jnp.float8_e4m3fn
I8 = jnp.int8
NT_DIMS = (((1,), (1,)), ((), ()))
LANES = 128
MESH = pl.DeviceIdType.MESH
GROUPS = 19
EARLY = 4
ROWS = 21
VMEM_LIMIT = 60 * 2**20


def list_rows(core, nb_ref, cnt_col, hi_ref, lo_ref):
    nb = nb_ref[...]
    valid = lax.broadcasted_iota(jnp.int32, nb.shape, 1).astype(F32) < cnt_col
    segment = lax.shift_right_logical(nb, 13)
    chip = lax.bitwise_and(lax.shift_right_logical(nb, 7), 63)
    source_core = lax.bitwise_and(lax.shift_right_logical(nb, 6), 1)
    slot = chip_slot(lax.shift_right_logical(chip, 4), lax.bitwise_and(lax.shift_right_logical(chip, 2), 3), lax.bitwise_and(chip, 3))
    is_halo = segment == 2 * core
    half = segment - 1 + core
    hi = slot + jnp.where(is_halo, 64, jnp.where(source_core == core, -64, 0))
    lo = jnp.where(is_halo, lax.bitwise_and(nb, 127), lax.bitwise_and(nb, 63) + 64 * half)
    hi_ref[...] = jnp.where(valid, hi, -128)
    lo_ref[...] = lo


def chip_slot(x, z, y):
    return lax.bitwise_and(x + z + y, 3) * 16 + x * 4 + y


def count_nodes(step, hi_ref, lo_ref, tmp_ref, last_ref, m_ref):
    fan = hi_ref.shape[1]
    tiles = tmp_ref.shape[1]
    hi_ids = (lax.broadcasted_iota(jnp.int32, (tiles, fan), 0) - 64).astype(I8)
    lo_ids = lax.broadcasted_iota(jnp.int32, (LANES, fan), 0).astype(I8)
    one, zero = jnp.ones((), E4), jnp.zeros((), E4)
    for i in range(8):
        n = step * 8 + i
        hi = jnp.broadcast_to(hi_ref[pl.ds(n, 1), :], (32, fan)).astype(I8)
        lo = jnp.broadcast_to(lo_ref[pl.ds(n, 1), :], (32, fan)).astype(I8)
        hot_hi = jnp.where(hi_ids == jnp.concatenate([hi] * (tiles // 32), 0), one, zero)
        hot_lo = jnp.where(lo_ids == jnp.concatenate([lo] * (LANES // 32), 0), one, zero)
        tmp_ref[i] = lax.dot_general(hot_hi, hot_lo, NT_DIMS, preferred_element_type=F32)
        if last_ref is not None:
            place_counts(step - 1, last_ref, m_ref, i * tiles // 8, (i + 1) * tiles // 8)


def place_counts(step, tmp_ref, m_ref, first, stop):
    m_ref[first:stop, pl.ds(pl.multiple_of(step * 8, 8), 8), :] = jnp.swapaxes(tmp_ref[:, first:stop, :], 0, 1)


def split2(x):
    high = x.astype(BF)
    return high, (x - high.astype(F32)).astype(BF)


def split3(x):
    high = x.astype(BF)
    rest = x - high.astype(F32)
    mid = rest.astype(BF)
    return high, mid, (rest - mid.astype(F32)).astype(BF)


def node_left(node_x, node_y, node_z):
    scale = 8.0 * math.log2(math.e)
    col = lax.broadcasted_iota(jnp.int32, (node_x.shape[0], LANES), 1)
    row = lax.bitwise_and(col, 7)
    vals = jnp.where(
        row == 0,
        node_x * scale,
        jnp.where(row == 1, node_y * scale, jnp.where(row == 2, node_z * scale, jnp.where(row == 3, -scale, 0.0))),
    )
    high, mid, low = split3(vals)
    block = lax.shift_right_logical(col, 3)
    high, mid, low = high.astype(F32), mid.astype(F32), low.astype(F32)
    part = jnp.where(
        (block == 0) | (block == 3) | (block == 5),
        high,
        jnp.where((block == 1) | (block == 4), mid, jnp.where(block == 2, low, 0.0)),
    )
    return part.astype(BF)


def meta_features(meta):
    dense = jnp.swapaxes(meta, 0, 1)
    y, z, c, s = (dense[i] for i in range(4))
    x = jnp.sqrt(jnp.maximum(1.0 - y * y - z * z, 0.0))
    one, zero = jnp.ones_like(x), jnp.zeros_like(x)
    rows = jnp.swapaxes(jnp.stack([x, y, z, one, c, s, zero, zero], 0), 0, 1)
    products = [x, y, z, c, s, x * x, x * y, x * z, y * y, y * z, x * c, y * c, z * c, x * s, y * s, z * s, c * c, c * s]
    return products, rows


def build_block(blk, level_base, ext_ref, gh_ref, gl_ref, fh_ref, fl_ref):
    start = pl.multiple_of(blk * 8, 8)
    meta = ext_ref[pl.ds(start, 8), 16:24, :]
    products, features = meta_features(meta)
    for t in range(8):
        gh_ref[GROUPS - 1 + t] = features[t]
    for index, prod in enumerate(products):
        high = prod.astype(BF).astype(F32)
        gh_ref[index] = high
        gl_ref[index] = prod - high
    level = (lax.broadcasted_iota(jnp.int32, (8, LANES), 0) + level_base).astype(F32)
    zero, one = jnp.zeros((8, LANES), F32), jnp.ones((8, LANES), F32)
    parts = []
    for t in range(8):
        rows = ext_ref[start + t]
        depth = jnp.broadcast_to(rows[20:21], (8, LANES))
        inside = level < depth
        hold = jnp.where(inside, one, zero)
        high, mid, low = split3(features[t])
        high, mid, low = high.astype(F32), mid.astype(F32), low.astype(F32)
        parts.append(jnp.concatenate([high, high, high, mid, mid, low], 0).astype(BF))
        for g_ref, f_ref, first in ((gh_ref, fh_ref, hold), (gl_ref, fl_ref, zero)):
            terms = [jnp.where(inside, jnp.broadcast_to(g_ref[i, t : t + 1, :], (8, LANES)), zero) for i in range(GROUPS - 1)]
            terms = [first] + terms + [zero]
            for pair in range(10):
                f_ref[t, pl.ds(pair * 16, 16)] = jnp.concatenate(terms[2 * pair : 2 * pair + 2], 0).astype(BF)
        factors = [jnp.broadcast_to(gh_ref[GROUPS - 1 + t, i : i + 1, :], (8, LANES)) for i in (0, 1, 2, 4, 5)]
        for v in range(2):
            value = jnp.where(inside, rows[8 * v : 8 * v + 8], zero)
            terms = [value] + [value * factor for factor in factors]
            for pair in range(3):
                both = jnp.concatenate(terms[2 * pair : 2 * pair + 2], 0)
                high = both.astype(BF)
                part = pl.ds((10 + 3 * v + pair) * 16, 16)
                fh_ref[t, part] = high
                fl_ref[t, part] = (both - high.astype(F32)).astype(BF)
    return jnp.concatenate(parts, 1)


def weigh_block(right, blk, m_ref, left, w_ref):
    nodes = m_ref.shape[1]
    start = pl.multiple_of(blk * 8, 8)
    power = lax.dot_general(left[:, :48], right, (((1,), (0,)), ((), ())), preferred_element_type=F32)
    for t in range(8):
        w_high, w_low = split2(jnp.exp2(power[:, t * LANES : (t + 1) * LANES]) * m_ref[start + t])
        w_ref[t, 0:nodes] = w_high
        w_ref[t, nodes:] = w_low


def add_block(fh_ref, fl_ref, w_ref, acc_ref):
    nodes = acc_ref.shape[0]
    def wide(ref, rows):
        return jnp.concatenate([ref[t, 0:rows] for t in range(8)], 1)

    first = lax.dot_general(wide(w_ref, 2 * nodes), wide(fh_ref, 256), NT_DIMS, preferred_element_type=F32)
    second = lax.dot_general(wide(w_ref, nodes), wide(fl_ref, 256), NT_DIMS, preferred_element_type=F32)
    acc_ref[...] += first[:nodes] + first[nodes:] + second


def fit_nodes(acc_ref, frame, out_ref):
    nodes = acc_ref.shape[0]
    columns = acc_ref[...].T
    ex, ey, qx, qy, qz = (jnp.broadcast_to(2.0 * part, (8, nodes)) for part in frame)
    sums = [columns[8 * i : 8 * i + 8, :] for i in range(32)]
    del sums[GROUPS]
    s1, sx, sy, sz, sc, ss, sxx, sxy, sxz, syy, syz, sxc, syc, szc, sxs, sys_, szs, scc, scs = sums[:GROUPS]
    szz = s1 - sxx - syy
    normal = {
        (0, 0): s1,
        (0, 1): ex * sx + ey * sy,
        (0, 2): qx * sx + qy * sy + qz * sz,
        (0, 3): sc,
        (0, 4): ss,
        (1, 1): ex * ex * sxx + 2.0 * ex * ey * sxy + ey * ey * syy,
        (1, 2): ex * qx * sxx + (ex * qy + ey * qx) * sxy + ey * qy * syy + ex * qz * sxz + ey * qz * syz,
        (1, 3): ex * sxc + ey * syc,
        (1, 4): ex * sxs + ey * sys_,
        (2, 2): qx * qx * sxx + qy * qy * syy + qz * qz * szz + 2.0 * (qx * qy * sxy + qx * qz * sxz + qy * qz * syz),
        (2, 3): qx * sxc + qy * syc + qz * szc,
        (2, 4): qx * sxs + qy * sys_ + qz * szs,
        (3, 3): scc,
        (3, 4): scs,
        (4, 4): s1 - scc,
    }
    lower = {}
    inverse = []
    for column in range(5):
        diagonal = normal[column, column] + 1.0
        for inner in range(column):
            diagonal = diagonal - lower[column, inner] * lower[column, inner]
        inverse.append(1.0 / jnp.sqrt(diagonal))
        for target in range(column + 1, 5):
            element = normal[column, target]
            for inner in range(column):
                element = element - lower[target, inner] * lower[column, inner]
            lower[target, column] = element * inverse[column]
    for v in range(2):
        m1, mx, my, mz, mc, ms = sums[GROUPS + 6 * v : GROUPS + 6 * v + 6]
        moments = [m1, ex * mx + ey * my, qx * mx + qy * my + qz * mz, mc, ms]
        forward = []
        for target in range(5):
            residue = moments[target]
            for inner in range(target):
                residue = residue - lower[target, inner] * forward[inner]
            forward.append(residue * inverse[target])
        coeffs = [None] * 5
        for target in reversed(range(5)):
            residue = forward[target]
            for inner in range(target + 1, 5):
                residue = residue - lower[inner, target] * coeffs[inner]
            coeffs[target] = residue * inverse[target]
        out_ref[v] = coeffs[0] + coeffs[3] * math.cos(MONTH_ANGLE) + coeffs[4] * math.sin(MONTH_ANGLE)


def node_frame(longitude, latitude):
    sin_lat, cos_lat = jnp.sin(latitude), jnp.cos(latitude)
    sin_lon, cos_lon = jnp.sin(longitude), jnp.cos(longitude)
    point = (cos_lat * cos_lon, cos_lat * sin_lon, sin_lat)
    frame = (-sin_lon, cos_lon, -sin_lat * cos_lon, -sin_lat * sin_lon, cos_lat)
    return point, frame


def dense_rows(ref, row):
    return jnp.concatenate([ref[row : row + 1, m * LANES : (m + 1) * LANES] for m in range(ref.shape[1] // LANES)], 0)


def profile_meta(place_ref, depth_ref):
    longitude, latitude, day_angle = (dense_rows(place_ref, row) for row in range(3))
    pair = lax.broadcasted_iota(jnp.int32, longitude.shape, 0).astype(F32)
    longitude = longitude - (pair * (math.pi / 8) + (math.pi / 16 - math.pi))
    cos_lat = jnp.cos(latitude)
    rows = [
        cos_lat * jnp.sin(longitude),
        jnp.sin(latitude),
        jnp.cos(day_angle),
        jnp.sin(day_angle),
        dense_rows(depth_ref, 0).astype(F32),
        cos_lat * jnp.cos(longitude),
        jnp.zeros_like(cos_lat),
        jnp.zeros_like(cos_lat),
    ]
    return jnp.swapaxes(jnp.stack(rows, 0), 0, 1)


def compute(nodes, level_base, early, start, before_count, before_pair, left, ext_ref, hi_ref, lo_ref, m_ref, work):
    tmp_a, tmp_b, gh_a, gl_a, gh_b, gl_b, fh_a, fl_a, w_a, fh_b, fl_b, w_b, acc_ref = work
    acc_ref[...] = jnp.zeros_like(acc_ref)
    def count_group(step, odd):
        now, last = (tmp_b, tmp_a) if odd else (tmp_a, tmp_b)
        count_nodes(step, hi_ref, lo_ref, now, last, m_ref)

    count_nodes(0, hi_ref, lo_ref, tmp_a, None, None)
    for step in range(1, early):
        count_group(step, step % 2 == 1)
    start()

    def count_step(step, carry):
        before_count(step)
        for i in range(4):
            count_group(early + 4 * step + i, (early + i) % 2 == 1)
        return carry

    rounds = (nodes // 8 - early) // 4
    lax.fori_loop(0, rounds, count_step, 0)
    for step in range(early + 4 * rounds, nodes // 8):
        count_group(step, step % 2 == 1)
    place_counts(nodes // 8 - 1, tmp_b, m_ref, 0, m_ref.shape[0])

    def build(blk, gh_ref, gl_ref, fh_ref, fl_ref, w_ref):
        right = build_block(blk, level_base, ext_ref, gh_ref, gl_ref, fh_ref, fl_ref)
        weigh_block(right, blk, m_ref, left, w_ref)

    set_a = (gh_a, gl_a, fh_a, fl_a, w_a)
    set_b = (gh_b, gl_b, fh_b, fl_b, w_b)
    index = before_pair(0)
    build(2 * index, *set_a)

    def pair_step(pair, index):
        following = before_pair(pair + 1)
        build(2 * index + 1, *set_b)
        add_block(fh_a, fl_a, w_a, acc_ref)
        build(2 * following, *set_a)
        add_block(fh_b, fl_b, w_b, acc_ref)
        return following

    pairs = ext_ref.shape[0] // 16
    index = lax.fori_loop(0, pairs - 1, pair_step, index)
    build(2 * index + 1, *set_b)
    add_block(fh_a, fl_a, w_a, acc_ref)
    add_block(fh_b, fl_b, w_b, acc_ref)


def work_buffers(nodes):
    tile = pltpu.VMEM((8, 192, LANES), F32)
    dense = pltpu.VMEM((GROUPS + 7, 8, LANES), F32)
    wide = pltpu.VMEM((8, 256, LANES), BF)
    return (tile, tile) + (dense,) * 4 + (wide,) * 6 + (pltpu.VMEM((nodes, 256), F32),)


def full_kernel(
    values_hbm, place_ref, depth_ref, node_ref, nb_hbm, cnt_ref, out_ref,
    values_ref, nb_ref,
    meta_ref, sib_values_ref, sib_meta_ref, own_ref, halo_ref, ext_ref,
    hi_ref, lo_ref, m_ref, work,
    send_own, send_halo, recv, pass_send, sib_send, sib_recv, load_sem,
):
    x = lax.axis_index("band")
    tile = lax.axis_index("tile")
    core = lax.rem(tile, 2)
    chip = lax.div(tile, 2)
    z, y = lax.div(chip, 4), lax.rem(chip, 4)
    sibling = {"tile": tile + 1 - 2 * core}
    mine = chip_slot(x, z, y)
    phase = lax.rem(x + z + y, 4)
    nodes = nb_ref.shape[0]

    def partner(index):
        dx, dy = lax.bitwise_and(lax.shift_right_logical(index, 2), 3), lax.bitwise_and(index, 3)
        dz = lax.shift_right_logical(index, 4) + 8 - dx - dy
        other_x, other_z, other_y = lax.bitwise_and(x + dx, 3), lax.bitwise_and(z + dz, 3), lax.bitwise_and(y + dy, 3)
        pair = other_z * 4 + other_y
        return other_x * 16 + pair, {"band": other_x, "tile": 2 * pair + core}

    loads = [
        pltpu.make_async_copy(values_hbm, values_ref, load_sem.at[0]),
        pltpu.make_async_copy(nb_hbm, nb_ref, load_sem.at[1]),
    ]
    for load in loads:
        load.start()
    barrier = pltpu.get_barrier_semaphore()

    def greet(index, carry):
        _, device = partner(index + 1)
        pl.semaphore_signal(barrier, inc=1, device_id=device, device_id_type=MESH)
        return carry

    lax.fori_loop(0, 63, greet, 0, unroll=7)
    pl.semaphore_signal(barrier, inc=1, device_id=sibling, device_id_type=MESH)

    meta_ref[...] = profile_meta(place_ref, depth_ref)
    loads[0].wait()
    for b in range(4):
        for m in range(16):
            for v in range(2):
                own_ref[b * 16 + m, 8 * v : 8 * v + 8, :] = values_ref[v, 8 * b : 8 * b + 8, m * LANES : (m + 1) * LANES]
            own_ref[b * 16 + m, 16:24, :] = meta_ref[m]
    middle = jnp.full((1, nodes), chip, jnp.int32).astype(F32) * (math.pi / 8) + (math.pi / 16 - math.pi)
    point, frame = node_frame(node_ref[0:1, :] - middle, node_ref[1:2, :])
    packed = jnp.concatenate(list(point) + [cnt_ref[...].astype(F32)] + [jnp.zeros((124, nodes), F32)], 0)
    columns = packed.T
    left = node_left(columns[:, 0:1], columns[:, 1:2], columns[:, 2:3])
    loads[1].wait()
    list_rows(core, nb_ref, columns[:, 3:4], hi_ref, lo_ref)

    sib_copies = [
        pltpu.make_async_remote_copy(values_ref, sib_values_ref, sib_send.at[0], sib_recv.at[0], device_id=sibling, device_id_type=MESH),
        pltpu.make_async_remote_copy(meta_ref, sib_meta_ref, sib_send.at[1], sib_recv.at[1], device_id=sibling, device_id_type=MESH),
    ]

    def send(buffer, base, send_sem):
        def step(index, carry):
            unit, device = partner(index + 1)
            pltpu.make_async_remote_copy(
                buffer.at[unit, pl.ds(0, ROWS)], ext_ref.at[16 * base + mine, pl.ds(0, ROWS)], send_sem, recv.at[base + phase], device_id=device, device_id_type=MESH
            ).start()
            return carry

        lax.fori_loop(0, 63, step, 0, unroll=7)

    def keep(buffer, base):
        return pltpu.make_async_copy(buffer.at[x * 16 + chip, pl.ds(0, ROWS)], ext_ref.at[16 * base + mine, pl.ds(0, ROWS)], recv.at[base + phase])

    def group(index):
        return ext_ref.at[pl.ds(pl.multiple_of(index * 16, 16), 16), pl.ds(0, ROWS)]

    def wait_group(index):
        pltpu.make_async_copy(group(index), group(index), recv.at[index]).wait()

    def start():
        pl.semaphore_wait(barrier, 64)
        for copy in sib_copies:
            copy.start()
        keep(own_ref, 0).start()
        send(own_ref, 0, send_own)

    def send_halos():
        for copy in sib_copies:
            copy.wait_recv()
        turn = jnp.full((1, LANES), 2 * core - 1, jnp.int32).astype(F32) * math.sin(math.pi / 8)
        first_row = lax.broadcasted_iota(jnp.int32, (8, LANES), 0) == 0
        from_own = lax.shift_right_logical(lax.broadcasted_iota(jnp.int32, (8, LANES), 1), 6) == core

        def step(m, carry):
            other = lax.rem(m + 15 + 2 * core, 16)
            cols = pl.ds(pl.multiple_of(other * LANES, LANES), LANES)
            meta = jnp.where(from_own, pltpu.roll(meta_ref[other], 64, 1), sib_meta_ref[other])
            turned = meta[0:1] * math.cos(math.pi / 8) + meta[5:6] * turn
            meta = jnp.where(first_row, jnp.broadcast_to(turned, (8, LANES)), meta)
            for b in range(4):
                unit = b * 16 + m
                for v in range(2):
                    mine_rows = values_ref[v, 8 * b : 8 * b + 8, cols]
                    their_rows = sib_values_ref[v, 8 * b : 8 * b + 8, cols]
                    halo_ref[unit, 8 * v : 8 * v + 8, :] = jnp.where(from_own, pltpu.roll(mine_rows, 64, 1), their_rows)
                halo_ref[unit, 16:24, :] = meta
            return carry

        lax.fori_loop(0, 16, step, 0)
        keep(halo_ref, 8).start()
        send(halo_ref, 8, send_halo)

    def pass_copy(k):
        return pltpu.make_async_remote_copy(
            group(k), group(4 + k), pass_send.at[k], recv.at[4 + k], device_id=sibling, device_id_type=MESH
        )

    def before_count(step):
        pl.when(step == 1)(send_halos)

    def before_pair(pair):
        k = lax.bitwise_and(phase + 4 - pair, 3)
        index = pair - lax.bitwise_and(pair, 3) + k
        wait_group(index)
        pl.when(pair < 4)(lambda: pass_copy(k).start())
        return index

    compute(nodes, x * 8, EARLY, start, before_count, before_pair, left, ext_ref, hi_ref, lo_ref, m_ref, work)
    fit_nodes(work[-1], frame, out_ref)
    for buffer, send_sem in ((own_ref, send_own), (halo_ref, send_halo)):
        view = buffer.at[pl.ds(0, 63), pl.ds(0, ROWS)]
        pltpu.make_async_copy(view, view, send_sem).wait()
    for k in range(4):
        pass_copy(k).wait_send()
    for copy in sib_copies:
        copy.wait_send()


def body(obs_values, obs_place, obs_depth, node_place, neighbours, counts):
    nodes, fan = neighbours.shape
    vmem = pl.BlockSpec(memory_space=pltpu.VMEM)
    hbm = pl.BlockSpec(memory_space=pl.ANY)
    dma = pltpu.SemaphoreType.DMA
    return pl.pallas_call(
        full_kernel,
        out_shape=jax.ShapeDtypeStruct((2, 8, nodes), F32),
        in_specs=[hbm, vmem, vmem, vmem, hbm, vmem],
        out_specs=vmem,
        scratch_shapes=[
            pltpu.VMEM(obs_values.shape, F32),
            pltpu.VMEM((nodes, fan), jnp.int32),
            pltpu.VMEM((16, 8, LANES), F32),
            pltpu.VMEM(obs_values.shape, F32),
            pltpu.VMEM((16, 8, LANES), F32),
            pltpu.VMEM((64, 24, LANES), F32),
            pltpu.VMEM((64, 24, LANES), F32),
            pltpu.VMEM((192, 24, LANES), F32),
            pltpu.VMEM((nodes, fan), jnp.int32),
            pltpu.VMEM((nodes, fan), jnp.int32),
            pltpu.VMEM((192, nodes, LANES), F32),
            work_buffers(nodes),
            dma,
            dma,
            dma((12,)),
            dma((4,)),
            dma((2,)),
            dma((2,)),
            dma((2,)),
        ],
        compiler_params=pltpu.CompilerParams(vmem_limit_bytes=VMEM_LIMIT, collective_id=0, has_side_effects=True),
    )(obs_values, obs_place, obs_depth.reshape(1, -1), node_place, neighbours, counts.reshape(1, nodes))


def solution(mesh):
    return jax.shard_map(
        body,
        mesh=mesh,
        in_specs=(
            P(None, None, ("band", "tile")),
            P(None, ("band", "tile")),
            P(("band", "tile")),
            P(None, "tile"),
            P("tile", None),
            P("tile"),
        ),
        out_specs=P(None, "band", "tile"),
        check_vma=False,
    )
```

```python
import math

import jax
import jax.numpy as jnp
from jax import lax
from jax.experimental import pallas as pl
from jax.experimental.pallas import tpu as pltpu
from jax.sharding import PartitionSpec as P

MONTH_ANGLE = -11.0 * math.pi / 12.0
BF = jnp.bfloat16
F32 = jnp.float32
E4 = jnp.float8_e4m3fn
I8 = jnp.int8
NT_DIMS = (((1,), (1,)), ((), ()))
LANES = 128
MESH = pl.DeviceIdType.MESH
LOGICAL = pl.DeviceIdType.LOGICAL
GROUPS = 19
EARLY = 3
ROWS = 21
VMEM_LIMIT = 60 * 2**20


def list_rows(core, nb_ref, cnt_col, hi_ref, lo_ref):
    nb = nb_ref[...]
    valid = lax.broadcasted_iota(jnp.int32, nb.shape, 1).astype(F32) < cnt_col
    segment = lax.shift_right_logical(nb, 13)
    chip = lax.bitwise_and(lax.shift_right_logical(nb, 7), 63)
    source_core = lax.bitwise_and(lax.shift_right_logical(nb, 6), 1)
    slot = chip_slot(lax.shift_right_logical(chip, 4), lax.bitwise_and(lax.shift_right_logical(chip, 2), 3), lax.bitwise_and(chip, 3))
    is_halo = segment == 2 * core
    half = segment - 1 + core
    hi = slot + jnp.where(is_halo, 64, jnp.where(source_core == core, -64, 0))
    lo = jnp.where(is_halo, lax.bitwise_and(nb, 127), lax.bitwise_and(nb, 63) + 64 * half)
    hi_ref[...] = jnp.where(valid, hi, -128)
    lo_ref[...] = lo


def chip_slot(x, z, y):
    return lax.bitwise_and(x + z + y, 3) * 16 + x * 4 + y


def count_nodes(step, hi_ref, lo_ref, tmp_ref, last_ref, m_ref):
    fan = hi_ref.shape[1]
    tiles = tmp_ref.shape[1]
    hi_ids = (lax.broadcasted_iota(jnp.int32, (tiles, fan), 0) - 64).astype(I8)
    lo_ids = lax.broadcasted_iota(jnp.int32, (LANES, fan), 0).astype(I8)
    one, zero = jnp.ones((), E4), jnp.zeros((), E4)
    for i in range(8):
        n = step * 8 + i
        hi = jnp.broadcast_to(hi_ref[pl.ds(n, 1), :], (32, fan)).astype(I8)
        lo = jnp.broadcast_to(lo_ref[pl.ds(n, 1), :], (32, fan)).astype(I8)
        hot_hi = jnp.where(hi_ids == jnp.concatenate([hi] * (tiles // 32), 0), one, zero)
        hot_lo = jnp.where(lo_ids == jnp.concatenate([lo] * (LANES // 32), 0), one, zero)
        tmp_ref[i] = lax.dot_general(hot_hi, hot_lo, NT_DIMS, preferred_element_type=F32)
        if last_ref is not None:
            place_counts(step - 1, last_ref, m_ref, i * tiles // 8, (i + 1) * tiles // 8)


def place_counts(step, tmp_ref, m_ref, first, stop):
    m_ref[first:stop, pl.ds(pl.multiple_of(step * 8, 8), 8), :] = jnp.swapaxes(tmp_ref[:, first:stop, :], 0, 1)


def split2(x):
    high = x.astype(BF)
    return high, (x - high.astype(F32)).astype(BF)


def split3(x):
    high = x.astype(BF)
    rest = x - high.astype(F32)
    mid = rest.astype(BF)
    return high, mid, (rest - mid.astype(F32)).astype(BF)


def node_left(node_x, node_y, node_z):
    scale = 8.0 * math.log2(math.e)
    col = lax.broadcasted_iota(jnp.int32, (node_x.shape[0], LANES), 1)
    row = lax.bitwise_and(col, 7)
    vals = jnp.where(
        row == 0,
        node_x * scale,
        jnp.where(row == 1, node_y * scale, jnp.where(row == 2, node_z * scale, jnp.where(row == 3, -scale, 0.0))),
    )
    high, mid, low = split3(vals)
    block = lax.shift_right_logical(col, 3)
    high, mid, low = high.astype(F32), mid.astype(F32), low.astype(F32)
    part = jnp.where(
        (block == 0) | (block == 3) | (block == 5),
        high,
        jnp.where((block == 1) | (block == 4), mid, jnp.where(block == 2, low, 0.0)),
    )
    return part.astype(BF)


def meta_features(meta):
    dense = jnp.swapaxes(meta, 0, 1)
    y, z, c, s = (dense[i] for i in range(4))
    x = jnp.sqrt(jnp.maximum(1.0 - y * y - z * z, 0.0))
    one, zero = jnp.ones_like(x), jnp.zeros_like(x)
    rows = jnp.swapaxes(jnp.stack([x, y, z, one, c, s, zero, zero], 0), 0, 1)
    products = [x, y, z, c, s, x * x, x * y, x * z, y * y, y * z, x * c, y * c, z * c, x * s, y * s, z * s, c * c, c * s]
    return products, rows


def build_block(blk, level_base, ext_ref, gh_ref, gl_ref, fh_ref, fl_ref):
    start = pl.multiple_of(blk * 8, 8)
    meta = ext_ref[pl.ds(start, 8), 16:24, :]
    products, features = meta_features(meta)
    for t in range(8):
        gh_ref[GROUPS - 1 + t] = features[t]
    for index, prod in enumerate(products):
        high = prod.astype(BF).astype(F32)
        gh_ref[index] = high
        gl_ref[index] = prod - high
    level = (lax.broadcasted_iota(jnp.int32, (8, LANES), 0) + level_base).astype(F32)
    zero, one = jnp.zeros((8, LANES), F32), jnp.ones((8, LANES), F32)
    parts = []
    for t in range(8):
        rows = ext_ref[start + t]
        depth = jnp.broadcast_to(rows[20:21], (8, LANES))
        inside = level < depth
        hold = jnp.where(inside, one, zero)
        high, mid, low = split3(features[t])
        high, mid, low = high.astype(F32), mid.astype(F32), low.astype(F32)
        parts.append(jnp.concatenate([high, high, high, mid, mid, low], 0).astype(BF))
        for g_ref, f_ref, first in ((gh_ref, fh_ref, hold), (gl_ref, fl_ref, zero)):
            terms = [jnp.where(inside, jnp.broadcast_to(g_ref[i, t : t + 1, :], (8, LANES)), zero) for i in range(GROUPS - 1)]
            terms = [first] + terms + [zero]
            for pair in range(10):
                f_ref[t, pl.ds(pair * 16, 16)] = jnp.concatenate(terms[2 * pair : 2 * pair + 2], 0).astype(BF)
        factors = [jnp.broadcast_to(gh_ref[GROUPS - 1 + t, i : i + 1, :], (8, LANES)) for i in (0, 1, 2, 4, 5)]
        for v in range(2):
            value = jnp.where(inside, rows[8 * v : 8 * v + 8], zero)
            terms = [value] + [value * factor for factor in factors]
            for pair in range(3):
                both = jnp.concatenate(terms[2 * pair : 2 * pair + 2], 0)
                high = both.astype(BF)
                part = pl.ds((10 + 3 * v + pair) * 16, 16)
                fh_ref[t, part] = high
                fl_ref[t, part] = (both - high.astype(F32)).astype(BF)
    return jnp.concatenate(parts, 1)


def weigh_block(right, blk, m_ref, left, w_ref):
    nodes = m_ref.shape[1]
    start = pl.multiple_of(blk * 8, 8)
    power = lax.dot_general(left[:, :48], right, (((1,), (0,)), ((), ())), preferred_element_type=F32)
    for t in range(8):
        w_high, w_low = split2(jnp.exp2(power[:, t * LANES : (t + 1) * LANES]) * m_ref[start + t])
        w_ref[t, 0:nodes] = w_high
        w_ref[t, nodes:] = w_low


def add_block(fh_ref, fl_ref, w_ref, acc_ref):
    nodes = acc_ref.shape[0]
    def wide(ref, rows):
        return jnp.concatenate([ref[t, 0:rows] for t in range(8)], 1)

    first = lax.dot_general(wide(w_ref, 2 * nodes), wide(fh_ref, 256), NT_DIMS, preferred_element_type=F32)
    second = lax.dot_general(wide(w_ref, nodes), wide(fl_ref, 256), NT_DIMS, preferred_element_type=F32)
    acc_ref[...] += first[:nodes] + first[nodes:] + second


def fit_nodes(acc_ref, frame, out_ref):
    nodes = acc_ref.shape[0]
    columns = acc_ref[...].T
    ex, ey, qx, qy, qz = (jnp.broadcast_to(2.0 * part, (8, nodes)) for part in frame)
    sums = [columns[8 * i : 8 * i + 8, :] for i in range(32)]
    del sums[GROUPS]
    s1, sx, sy, sz, sc, ss, sxx, sxy, sxz, syy, syz, sxc, syc, szc, sxs, sys_, szs, scc, scs = sums[:GROUPS]
    szz = s1 - sxx - syy
    normal = {
        (0, 0): s1,
        (0, 1): ex * sx + ey * sy,
        (0, 2): qx * sx + qy * sy + qz * sz,
        (0, 3): sc,
        (0, 4): ss,
        (1, 1): ex * ex * sxx + 2.0 * ex * ey * sxy + ey * ey * syy,
        (1, 2): ex * qx * sxx + (ex * qy + ey * qx) * sxy + ey * qy * syy + ex * qz * sxz + ey * qz * syz,
        (1, 3): ex * sxc + ey * syc,
        (1, 4): ex * sxs + ey * sys_,
        (2, 2): qx * qx * sxx + qy * qy * syy + qz * qz * szz + 2.0 * (qx * qy * sxy + qx * qz * sxz + qy * qz * syz),
        (2, 3): qx * sxc + qy * syc + qz * szc,
        (2, 4): qx * sxs + qy * sys_ + qz * szs,
        (3, 3): scc,
        (3, 4): scs,
        (4, 4): s1 - scc,
    }
    lower = {}
    inverse = []
    for column in range(5):
        diagonal = normal[column, column] + 1.0
        for inner in range(column):
            diagonal = diagonal - lower[column, inner] * lower[column, inner]
        inverse.append(1.0 / jnp.sqrt(diagonal))
        for target in range(column + 1, 5):
            element = normal[column, target]
            for inner in range(column):
                element = element - lower[target, inner] * lower[column, inner]
            lower[target, column] = element * inverse[column]
    for v in range(2):
        m1, mx, my, mz, mc, ms = sums[GROUPS + 6 * v : GROUPS + 6 * v + 6]
        moments = [m1, ex * mx + ey * my, qx * mx + qy * my + qz * mz, mc, ms]
        forward = []
        for target in range(5):
            residue = moments[target]
            for inner in range(target):
                residue = residue - lower[target, inner] * forward[inner]
            forward.append(residue * inverse[target])
        coeffs = [None] * 5
        for target in reversed(range(5)):
            residue = forward[target]
            for inner in range(target + 1, 5):
                residue = residue - lower[inner, target] * coeffs[inner]
            coeffs[target] = residue * inverse[target]
        out_ref[v] = coeffs[0] + coeffs[3] * math.cos(MONTH_ANGLE) + coeffs[4] * math.sin(MONTH_ANGLE)


def node_frame(longitude, latitude):
    sin_lat, cos_lat = jnp.sin(latitude), jnp.cos(latitude)
    sin_lon, cos_lon = jnp.sin(longitude), jnp.cos(longitude)
    point = (cos_lat * cos_lon, cos_lat * sin_lon, sin_lat)
    frame = (-sin_lon, cos_lon, -sin_lat * cos_lon, -sin_lat * sin_lon, cos_lat)
    return point, frame


def dense_rows(ref, row):
    return jnp.concatenate([ref[row : row + 1, m * LANES : (m + 1) * LANES] for m in range(ref.shape[1] // LANES)], 0)


def profile_meta(place_ref, depth_ref):
    longitude, latitude, day_angle = (dense_rows(place_ref, row) for row in range(3))
    pair = lax.broadcasted_iota(jnp.int32, longitude.shape, 0).astype(F32)
    longitude = longitude - (pair * (math.pi / 8) + (math.pi / 16 - math.pi))
    cos_lat = jnp.cos(latitude)
    rows = [
        cos_lat * jnp.sin(longitude),
        jnp.sin(latitude),
        jnp.cos(day_angle),
        jnp.sin(day_angle),
        dense_rows(depth_ref, 0).astype(F32),
        cos_lat * jnp.cos(longitude),
        jnp.zeros_like(cos_lat),
        jnp.zeros_like(cos_lat),
    ]
    return jnp.swapaxes(jnp.stack(rows, 0), 0, 1)


def compute(nodes, level_base, early, start, before_count, before_pair, left, ext_ref, hi_ref, lo_ref, m_ref, work):
    tmp_a, tmp_b, gh_a, gl_a, gh_b, gl_b, fh_a, fl_a, w_a, fh_b, fl_b, w_b, acc_ref = work
    acc_ref[...] = jnp.zeros_like(acc_ref)
    def count_group(step, odd):
        now, last = (tmp_b, tmp_a) if odd else (tmp_a, tmp_b)
        count_nodes(step, hi_ref, lo_ref, now, last, m_ref)

    count_nodes(0, hi_ref, lo_ref, tmp_a, None, None)
    for step in range(1, early):
        count_group(step, step % 2 == 1)
    start()

    def count_step(step, carry):
        before_count(step)
        for i in range(4):
            count_group(early + 4 * step + i, (early + i) % 2 == 1)
        return carry

    rounds = (nodes // 8 - early) // 4
    lax.fori_loop(0, rounds, count_step, 0)
    for step in range(early + 4 * rounds, nodes // 8):
        count_group(step, step % 2 == 1)
    place_counts(nodes // 8 - 1, tmp_b, m_ref, 0, m_ref.shape[0])

    def build(blk, gh_ref, gl_ref, fh_ref, fl_ref, w_ref):
        right = build_block(blk, level_base, ext_ref, gh_ref, gl_ref, fh_ref, fl_ref)
        weigh_block(right, blk, m_ref, left, w_ref)

    set_a = (gh_a, gl_a, fh_a, fl_a, w_a)
    set_b = (gh_b, gl_b, fh_b, fl_b, w_b)
    index = before_pair(0)
    build(2 * index, *set_a)

    def pair_step(pair, index):
        following = before_pair(pair + 1)
        build(2 * index + 1, *set_b)
        add_block(fh_a, fl_a, w_a, acc_ref)
        build(2 * following, *set_a)
        add_block(fh_b, fl_b, w_b, acc_ref)
        return following

    pairs = ext_ref.shape[0] // 16
    index = lax.fori_loop(0, pairs - 1, pair_step, index)
    build(2 * index + 1, *set_b)
    add_block(fh_a, fl_a, w_a, acc_ref)
    add_block(fh_b, fl_b, w_b, acc_ref)


def work_buffers(nodes):
    tile = pltpu.VMEM((8, 192, LANES), F32)
    dense = pltpu.VMEM((GROUPS + 7, 8, LANES), F32)
    wide = pltpu.VMEM((8, 256, LANES), BF)
    return (tile, tile) + (dense,) * 4 + (wide,) * 6 + (pltpu.VMEM((nodes, 256), F32),)


def full_kernel(
    values_hbm, place_ref, depth_ref, node_ref, nb_hbm, cnt_ref, out_ref,
    values_ref, nb_ref,
    meta_ref, sib_values_ref, sib_meta_ref, own_ref, halo_ref, ext_ref,
    hi_ref, lo_ref, m_ref, work,
    send_own, send_halo, recv, pass_send, sib_send, sib_recv, load_sem,
):
    x = lax.axis_index("band")
    tile = lax.axis_index("tile")
    core = lax.rem(tile, 2)
    chip = lax.div(tile, 2)
    z, y = lax.div(chip, 4), lax.rem(chip, 4)
    sibling = {"tile": tile + 1 - 2 * core}
    mine = chip_slot(x, z, y)
    phase = lax.rem(x + z + y, 4)
    nodes = nb_ref.shape[0]

    def partner(index):
        dx, dy = lax.bitwise_and(lax.shift_right_logical(index, 2), 3), lax.bitwise_and(index, 3)
        dz = lax.shift_right_logical(index, 4) + 8 - dx - dy
        other_x, other_z, other_y = lax.bitwise_and(x + dx, 3), lax.bitwise_and(z + dz, 3), lax.bitwise_and(y + dy, 3)
        pair = other_z * 4 + other_y
        unit = other_x * 16 + pair
        return unit, 2 * unit + core

    loads = [
        pltpu.make_async_copy(values_hbm, values_ref, load_sem.at[0]),
        pltpu.make_async_copy(nb_hbm, nb_ref, load_sem.at[1]),
    ]
    for load in loads:
        load.start()
    barrier = pltpu.get_barrier_semaphore()

    def greet(index, carry):
        _, device = partner(index + 1)
        pl.semaphore_signal(barrier, inc=1, device_id=device, device_id_type=LOGICAL)
        return carry

    lax.fori_loop(0, 63, greet, 0, unroll=7)
    pl.semaphore_signal(barrier, inc=1, device_id=sibling, device_id_type=MESH)

    meta_ref[...] = profile_meta(place_ref, depth_ref)
    loads[0].wait()
    for b in range(4):
        for m in range(16):
            for v in range(2):
                own_ref[b * 16 + m, 8 * v : 8 * v + 8, :] = values_ref[v, 8 * b : 8 * b + 8, m * LANES : (m + 1) * LANES]
            own_ref[b * 16 + m, 16:24, :] = meta_ref[m]
    middle = jnp.full((1, nodes), chip, jnp.int32).astype(F32) * (math.pi / 8) + (math.pi / 16 - math.pi)
    point, frame = node_frame(node_ref[0:1, :] - middle, node_ref[1:2, :])
    packed = jnp.concatenate(list(point) + [cnt_ref[...].astype(F32)] + [jnp.zeros((124, nodes), F32)], 0)
    columns = packed.T
    left = node_left(columns[:, 0:1], columns[:, 1:2], columns[:, 2:3])
    loads[1].wait()
    list_rows(core, nb_ref, columns[:, 3:4], hi_ref, lo_ref)

    sib_copies = [
        pltpu.make_async_remote_copy(values_ref, sib_values_ref, sib_send.at[0], sib_recv.at[0], device_id=sibling, device_id_type=MESH),
        pltpu.make_async_remote_copy(meta_ref, sib_meta_ref, sib_send.at[1], sib_recv.at[1], device_id=sibling, device_id_type=MESH),
    ]

    def send(buffer, base, send_sem):
        def step(index, carry):
            unit, device = partner(index + 1)
            pltpu.make_async_remote_copy(
                buffer.at[unit, pl.ds(0, ROWS)], ext_ref.at[16 * base + mine, pl.ds(0, ROWS)], send_sem, recv.at[base + phase], device_id=device, device_id_type=LOGICAL
            ).start()
            return carry

        lax.fori_loop(0, 63, step, 0, unroll=7)

    def keep(buffer, base):
        return pltpu.make_async_copy(buffer.at[x * 16 + chip, pl.ds(0, ROWS)], ext_ref.at[16 * base + mine, pl.ds(0, ROWS)], recv.at[base + phase])

    def group(index):
        return ext_ref.at[pl.ds(pl.multiple_of(index * 16, 16), 16), pl.ds(0, ROWS)]

    def wait_group(index):
        pltpu.make_async_copy(group(index), group(index), recv.at[index]).wait()

    def start():
        pl.semaphore_wait(barrier, 64)
        for copy in sib_copies:
            copy.start()
        keep(own_ref, 0).start()
        send(own_ref, 0, send_own)

    def send_halos():
        for copy in sib_copies:
            copy.wait_recv()
        turn = jnp.full((1, LANES), 2 * core - 1, jnp.int32).astype(F32) * math.sin(math.pi / 8)
        first_row = lax.broadcasted_iota(jnp.int32, (8, LANES), 0) == 0
        from_own = lax.shift_right_logical(lax.broadcasted_iota(jnp.int32, (8, LANES), 1), 6) == core

        def step(m, carry):
            other = lax.rem(m + 15 + 2 * core, 16)
            cols = pl.ds(pl.multiple_of(other * LANES, LANES), LANES)
            meta = jnp.where(from_own, pltpu.roll(meta_ref[other], 64, 1), sib_meta_ref[other])
            turned = meta[0:1] * math.cos(math.pi / 8) + meta[5:6] * turn
            meta = jnp.where(first_row, jnp.broadcast_to(turned, (8, LANES)), meta)
            for b in range(4):
                unit = b * 16 + m
                for v in range(2):
                    mine_rows = values_ref[v, 8 * b : 8 * b + 8, cols]
                    their_rows = sib_values_ref[v, 8 * b : 8 * b + 8, cols]
                    halo_ref[unit, 8 * v : 8 * v + 8, :] = jnp.where(from_own, pltpu.roll(mine_rows, 64, 1), their_rows)
                halo_ref[unit, 16:24, :] = meta
            return carry

        lax.fori_loop(0, 16, step, 0)
        keep(halo_ref, 8).start()
        send(halo_ref, 8, send_halo)

    def pass_copy(k):
        return pltpu.make_async_remote_copy(
            group(k), group(4 + k), pass_send.at[k], recv.at[4 + k], device_id=sibling, device_id_type=MESH
        )

    def before_count(step):
        pl.when(step == 1)(send_halos)

    def before_pair(pair):
        k = lax.bitwise_and(phase + 4 - pair, 3)
        index = pair - lax.bitwise_and(pair, 3) + k
        wait_group(index)
        pl.when(pair < 4)(lambda: pass_copy(k).start())
        return index

    compute(nodes, x * 8, EARLY, start, before_count, before_pair, left, ext_ref, hi_ref, lo_ref, m_ref, work)
    fit_nodes(work[-1], frame, out_ref)
    for buffer, send_sem in ((own_ref, send_own), (halo_ref, send_halo)):
        view = buffer.at[pl.ds(0, 63), pl.ds(0, ROWS)]
        pltpu.make_async_copy(view, view, send_sem).wait()
    for k in range(4):
        pass_copy(k).wait_send()
    for copy in sib_copies:
        copy.wait_send()


def body(obs_values, obs_place, obs_depth, node_place, neighbours, counts):
    nodes, fan = neighbours.shape
    vmem = pl.BlockSpec(memory_space=pltpu.VMEM)
    hbm = pl.BlockSpec(memory_space=pl.ANY)
    dma = pltpu.SemaphoreType.DMA
    return pl.pallas_call(
        full_kernel,
        out_shape=jax.ShapeDtypeStruct((2, 8, nodes), F32),
        in_specs=[hbm, vmem, vmem, vmem, hbm, vmem],
        out_specs=vmem,
        scratch_shapes=[
            pltpu.VMEM(obs_values.shape, F32),
            pltpu.VMEM((nodes, fan), jnp.int32),
            pltpu.VMEM((16, 8, LANES), F32),
            pltpu.VMEM(obs_values.shape, F32),
            pltpu.VMEM((16, 8, LANES), F32),
            pltpu.VMEM((64, 24, LANES), F32),
            pltpu.VMEM((64, 24, LANES), F32),
            pltpu.VMEM((192, 24, LANES), F32),
            pltpu.VMEM((nodes, fan), jnp.int32),
            pltpu.VMEM((nodes, fan), jnp.int32),
            pltpu.VMEM((192, nodes, LANES), F32),
            work_buffers(nodes),
            dma,
            dma,
            dma((12,)),
            dma((4,)),
            dma((2,)),
            dma((2,)),
            dma((2,)),
        ],
        compiler_params=pltpu.CompilerParams(vmem_limit_bytes=VMEM_LIMIT, collective_id=0, has_side_effects=True),
    )(obs_values, obs_place, obs_depth.reshape(1, -1), node_place, neighbours, counts.reshape(1, nodes))


def solution(mesh):
    return jax.shard_map(
        body,
        mesh=mesh,
        in_specs=(
            P(None, None, ("band", "tile")),
            P(None, ("band", "tile")),
            P(("band", "tile")),
            P(None, "tile"),
            P("tile", None),
            P("tile"),
        ),
        out_specs=P(None, "band", "tile"),
        check_vma=False,
    )
```
